512 devices in a mesh: atoms: 16 (over z), pivots: 32 (over y, x, core).
Axes of the slice: x: 4, y: 4, z: 16, core: 2. Of those that a mesh axis runs over, the one named last changes fastest.
Arguments:
- descriptors: bfloat16 [16384, 2048], P('atoms', 'pivots'), may hold values from -6 to 6
- pivot_desc: bfloat16 [32768, 2048], P('pivots'), may hold values from -6 to 6
- coeffs: float32 [32768, 64], P('pivots'), may hold values from -0.00390625 to 0.00390625
- seg_ids: int32 [16, 1024], P('atoms'), may hold values from 0 to 127, never falling along the last dimension, each value on 1 to 24 neighbouring positions
- dest: int32 [2048], replicated, may hold values from 0 to 2047, as said below
- targets: float32 [2048, 64], P('atoms'), may hold values from -6 to 6
- weights: float32 [2048], P('atoms'), may hold values from 0.5 to 2
Outputs:
- residual: float32 [2048, 64], P('atoms', 'pivots')
- gradient: float32 [64, 32768], P('atoms', 'pivots')
The draws below stay inside these ranges and needn't reach their ends.
Inputs may be any that keep to these rules, and one draw needn't show every extreme that they name: dest is a permutation; the structures of home a (indices a * 128 to a * 128 + 127) go to owners dest // 128; at most 32 structures of one home go to one owner, some home sends exactly 32 to one owner, and every owner receives exactly 128. `seg_ids`: row a numbers the structure of each atom of home a; numbers never fall along a row and every number appears.
All inputs are finite; a program needn't handle non-finite values.
Results may differ from the reference program's by a relative error of at most 0.0011.
Values may be sent and summed in bfloat16 or wider, within the bound.
A program may use at most 64 MiB of HBM per device.

```python
import math
import jax
import jax.numpy as jnp
import numpy as np
from jax import lax

DESC = 2048
TARGETS = 64
ATOM_DEV = 1024
STRUCT_DEV = 128
CAP = 32
SHARDS = 16
ATOMS = 16384
PIVOTS = 32768
STRUCTS = 2048


def draw_dest(key, part):
    shard_count = SHARDS
    remainder = STRUCT_DEV - CAP
    weight_list = [CAP] + [remainder // (shard_count - 1) + (1 if index < remainder % (shard_count - 1) else 0) for index in range(shard_count - 1)]
    group_of_slot = np.repeat(np.arange(shard_count), weight_list).astype(np.int32)
    key_offset, key_label, key_shuffle, key_order = jax.random.split(key, 4)
    offsets = jax.random.permutation(key_offset, shard_count).astype(jnp.int32)
    relabel = jax.random.permutation(key_label, shard_count).astype(jnp.int32)
    home_index = jnp.arange(shard_count, dtype=jnp.int32)[:, None]
    owner_map = relabel[(home_index + offsets[jnp.asarray(group_of_slot)][None, :]) % shard_count]
    row_keys = jax.random.split(key_shuffle, shard_count)
    shuffled = jax.vmap(lambda row_key, row_data: jax.random.permutation(row_key, row_data))(row_keys, owner_map)
    owner_flat = shuffled.reshape(-1).astype(jnp.int32)
    priority = jax.random.permutation(key_order, shard_count * STRUCT_DEV).astype(jnp.int32)
    same_owner = owner_flat[:, None] == owner_flat[None, :]
    earlier = priority[None, :] < priority[:, None]
    ranking = jnp.sum((same_owner & earlier).astype(jnp.int32), axis=1)
    return (owner_flat * STRUCT_DEV + ranking).astype(jnp.int32)


def levels(rng, extent, shards, smallest, largest):
    def one(dim, blocks):
        steps = jax.random.uniform(jax.random.fold_in(jax.random.fold_in(rng, 6), dim), (blocks,), jnp.float32, smallest / len(shards), largest / len(shards))
        return jnp.repeat(jnp.exp(steps), extent[dim] // blocks).reshape((-1,) + (1,) * (len(extent) - dim - 1))

    gain = one(*shards[0])
    for cut in shards[1:]:
        gain = gain * one(*cut)
    return gain


def length_profile(amount, total, most, skew):
    loads = [(1 << 20) // math.isqrt(grade ** skew) + 1 for grade in range(2, amount + 1)]
    spare, holding = total - most - (amount - 1), [1] * (amount - 1)
    while spare > 0:
        free = [i for i in range(amount - 1) if holding[i] < most]
        pool, left = sum([loads[i] for i in free]), spare
        for i in free:
            more = min(most - holding[i], max(1, left * loads[i] // pool), spare)
            holding[i] = holding[i] + more
            spare = spare - more
    return np.array([most] + holding)


def uneven(key, amount, total, reach, slope):
    if amount == 2:
        one = jax.random.randint(key, (), max(1, total - reach), min(reach, total - 1) + 1)
        return jnp.stack([one, total - one])
    sizes = jnp.asarray(length_profile(amount, total, reach, slope), jnp.int32)
    couples = (amount - 1) // 2
    donor, receiver = sizes[1:1 + 2 * couples:2], sizes[2:2 + 2 * couples:2]
    slack = jnp.minimum(donor - 1, reach - receiver)
    shifted = jax.random.randint(jax.random.fold_in(key, 1), (couples,), 0, 1 << 20) % (slack + 1)
    sizes = sizes.at[1:1 + 2 * couples:2].set(donor - shifted).at[2:2 + 2 * couples:2].set(receiver + shifted)
    return sizes[jax.random.permutation(jax.random.fold_in(key, 2), amount)]


def scatter_about(stream_key, extent, width, bound, pieces=(), held_as=jnp.bfloat16):
    values = jax.random.normal(stream_key, extent, jnp.float32) * width
    if len(pieces) > 0:
        values = levels(stream_key, extent, pieces, -0.22, 0.18) * values
    return jnp.clip(values, min=-bound, max=bound).astype(held_as)


def setup_inputs(seed: int = 0) -> dict:
    key_list = jax.random.split(jax.random.key(seed), 8)
    return {
        "descriptors": scatter_about(key_list[0], (ATOMS, DESC), 1.0, 6.0, ((0, 16), (1, 32))),
        "pivot_desc": scatter_about(key_list[1], (PIVOTS, DESC), 1.0, 6.0, ((0, 32),)),
        "coeffs": scatter_about(key_list[2], (PIVOTS, TARGETS), (PIVOTS * (ATOM_DEV // STRUCT_DEV) ** 2) ** -0.5, 0.00390625, ((0, 32),), jnp.float32),
        "seg_ids": jax.vmap(lambda own: jnp.searchsorted(jnp.cumsum(uneven(own, STRUCT_DEV, ATOM_DEV, 3 * ATOM_DEV // STRUCT_DEV, 1)), jnp.arange(ATOM_DEV), side="right"))(jax.random.split(key_list[3], SHARDS)).reshape((SHARDS, ATOM_DEV)).astype(jnp.int32),
        "dest": draw_dest(jax.random.fold_in(key_list[7], 71), 0),
        "targets": scatter_about(key_list[5], (STRUCTS, TARGETS), 1.0, 6.0, ((0, 16),), jnp.float32),
        "weights": jnp.clip(jnp.exp(math.log(2.0) - 1.3862944 * jax.random.uniform(key_list[6], (STRUCTS,), jnp.float32) ** levels(key_list[6], (STRUCTS,), ((0, 16),), -0.2, 0.2)), 0.5, 2.0),
    }


eps = 1e-06

def reference(descriptors, pivot_desc, coeffs, seg_ids, dest, targets, weights):
    pivot_scale = lax.rsqrt(lax.optimization_barrier(jnp.sum(jnp.square(pivot_desc.astype(jnp.float32)), axis=1)) + eps)
    atom_blocks = descriptors.reshape(SHARDS, ATOM_DEV, DESC)

    def one_home(inputs):
        atom_rows, segment_row = inputs
        scores = jnp.dot(atom_rows, pivot_desc.T, preferred_element_type=jnp.float32)
        atom_scale = lax.rsqrt(lax.optimization_barrier(jnp.sum(jnp.square(atom_rows.astype(jnp.float32)), axis=1)) + eps)
        cosine = scores * atom_scale[:, None] * pivot_scale[None, :]
        kernel_tile = (DESC * jnp.square(cosine)).astype(jnp.bfloat16)
        members = (segment_row[None, :] == jnp.arange(STRUCT_DEV, dtype=jnp.int32)[:, None]).astype(jnp.bfloat16)
        return jnp.dot(members, kernel_tile, preferred_element_type=jnp.float32)
    structure_kernel = lax.map(one_home, (atom_blocks, seg_ids)).reshape(STRUCTS, PIVOTS)
    predicted = jnp.dot(structure_kernel, coeffs, precision=lax.Precision.HIGHEST, preferred_element_type=jnp.float32)
    target_home = targets[dest]
    weight_home = weights[dest]
    residual = weight_home[:, None] * (predicted - target_home)
    gradient = jnp.dot(residual.T, structure_kernel, precision=lax.Precision.HIGHEST, preferred_element_type=jnp.float32) / STRUCTS
    return (residual, gradient)
```

```python
import functools

import jax
import jax.numpy as jnp
from jax import lax
from jax.experimental import pallas as pl
from jax.experimental.pallas import tpu as pltpu
from jax.sharding import PartitionSpec as P

EPS = 1e-6
MESH = pl.DeviceIdType.MESH
F32 = jnp.float32
BF16 = jnp.bfloat16
NB = 4
NZ = 16
NX = 4


def split2(value):
    high = value.astype(BF16)
    low = (value - high.astype(F32)).astype(BF16)
    return high, low


def split3(value):
    high = value.astype(BF16)
    rest = value - high.astype(F32)
    mid = rest.astype(BF16)
    low = (rest - mid.astype(F32)).astype(BF16)
    return high, mid, low


def mm(left, right):
    return jnp.dot(left, right, preferred_element_type=F32)


def kernel(
    d_ref,
    p_ref,
    c_ref,
    seg_ref,
    dest_ref,
    tgt_ref,
    w_ref,
    res_ref,
    grad_ref,
    gathered,
    pv,
    cv,
    segv,
    destv,
    tgtv,
    wv,
    p2,
    members,
    skt,
    sht,
    slt,
    tz,
    pred_send,
    pred_recv,
    tiles,
    grad_send,
    grad_recv,
    arow,
    local_sem,
    own_sem,
    line_sem,
    half_sem,
    part_send_sem,
    recv_sem,
    part_recv_sem,
    z_send_sem,
    z_recv_sem,
    late_sem,
):
    z = lax.axis_index("atoms")
    p = lax.axis_index("pivots")
    c = lax.rem(p, 2)
    x = lax.rem(lax.div(p, 2), NX)
    y = lax.div(p, 2 * NX)
    q = lax.div(p, 4)
    rows = d_ref.shape[0]
    half = rows // 2
    atoms = d_ref.shape[1]
    width = atoms // NB
    pivots = p_ref.shape[0]
    tile = pivots // 4
    structs = tz.shape[2]

    def wrap(value):
        return lax.rem(value + NX, NX)

    def place(f, s):
        return wrap(y + s * (1 - c) + f * c), wrap(x + f * (1 - c) + s * c)

    def device(f, s):
        yi, xi = place(f, s)
        return (z, (yi * NX + xi) * 2 + c)

    partner = (z, p + 1 - 2 * c)
    up = (lax.rem(z + 1, NZ), p)
    down = (lax.rem(z + NZ - 1, NZ), p)
    f_up, f_down = device(1, 0), device(-1, 0)
    s_up, s_down = device(0, 1), device(0, -1)

    locals_ = [
        pltpu.make_async_copy(tgt_ref, tgtv, local_sem.at[0]),
        pltpu.make_async_copy(w_ref, wv, local_sem.at[1]),
        pltpu.make_async_copy(seg_ref, segv, local_sem.at[2]),
        pltpu.make_async_copy(p_ref, pv, local_sem.at[3]),
        pltpu.make_async_copy(c_ref, cv, local_sem.at[4]),
        pltpu.make_async_copy(dest_ref, destv, local_sem.at[5]),
        pltpu.make_async_copy(d_ref, gathered.at[y, x, c], local_sem.at[6]),
    ]
    barrier = pltpu.get_barrier_semaphore()
    for peer in (f_up, f_down, s_up, s_down, partner, up, down):
        pl.semaphore_signal(barrier, inc=1, device_id=peer, device_id_type=MESH)
    for copy in locals_:
        copy.start()
    pl.semaphore_wait(barrier, 7)

    def span(b):
        return pl.ds(pl.multiple_of(b * width, width), width)

    def own(b):
        for kind, peer in ((0, f_up), (1, f_down), (2, s_up), (3, s_down)):
            pltpu.make_async_remote_copy(
                src_ref=d_ref.at[:, span(b)],
                dst_ref=gathered.at[y, x, c, :, span(b)],
                send_sem=own_sem,
                recv_sem=recv_sem.at[kind, b],
                device_id=peer,
                device_id_type=MESH,
            ).start()
        pltpu.make_async_remote_copy(
            src_ref=d_ref.at[:, span(b)],
            dst_ref=gathered.at[y, x, c, :, span(b)],
            send_sem=part_send_sem,
            recv_sem=part_recv_sem.at[b],
            device_id=partner,
            device_id_type=MESH,
        ).start()

    for b in range(NB):
        own(b)

    def piece(spot, part, b):
        yi, xi = spot
        return gathered.at[yi, xi, c, part, span(b)]

    whole, low, high = pl.ds(0, rows), pl.ds(0, half), pl.ds(half, half)

    def forward(kind, b, spot, part, sem, peer):
        ref = piece(spot, part, b)
        pltpu.make_async_remote_copy(
            src_ref=ref,
            dst_ref=ref,
            send_sem=sem,
            recv_sem=recv_sem.at[kind, b],
            device_id=peer,
            device_id_type=MESH,
        ).start()

    def share(b, spot):
        ref = piece(spot, whole, b)
        pltpu.make_async_remote_copy(
            src_ref=ref,
            dst_ref=ref,
            send_sem=part_send_sem,
            recv_sem=part_recv_sem.at[b],
            device_id=partner,
            device_id_type=MESH,
        ).start()

    def arrive(kind, b, spot, part):
        ref = piece(spot, part, b)
        pltpu.make_async_remote_copy(
            src_ref=ref,
            dst_ref=ref,
            send_sem=own_sem,
            recv_sem=recv_sem.at[kind, b],
            device_id=partner,
            device_id_type=MESH,
        ).wait_recv()

    to_low, to_high = half_sem.at[0], half_sem.at[1]

    def event1(b):
        spot = place(-1, 0)
        arrive(0, b, spot, whole)
        forward(4, b, spot, low, to_low, f_up)
        forward(6, b, spot, whole, line_sem, s_up)
        forward(7, b, spot, whole, line_sem, s_down)
        share(b, spot)
        spot = place(1, 0)
        arrive(1, b, spot, whole)
        forward(5, b, spot, high, to_low, f_down)
        forward(8, b, spot, whole, line_sem, s_up)
        forward(9, b, spot, whole, line_sem, s_down)
        share(b, spot)
        spot = place(0, -1)
        arrive(2, b, spot, whole)
        forward(12, b, spot, low, to_high, s_up)
        share(b, spot)
        spot = place(0, 1)
        arrive(3, b, spot, whole)
        forward(13, b, spot, high, to_high, s_down)
        share(b, spot)

    def event2(b):
        spot = place(2, 0)
        arrive(4, b, spot, low)
        arrive(5, b, spot, high)
        forward(10, b, spot, whole, line_sem, s_up)
        forward(11, b, spot, whole, line_sem, s_down)
        share(b, spot)
        for f, first in ((-1, 6), (1, 8)):
            spot = place(f, -1)
            arrive(first, b, spot, whole)
            forward(first + 8, b, spot, low, to_high, s_up)
            share(b, spot)
            spot = place(f, 1)
            arrive(first + 1, b, spot, whole)
            forward(first + 9, b, spot, high, to_high, s_down)
            share(b, spot)
        spot = place(0, 2)
        arrive(12, b, spot, low)
        arrive(13, b, spot, high)
        share(b, spot)

    def event3(b):
        spot = place(2, -1)
        arrive(10, b, spot, whole)
        forward(18, b, spot, low, to_high, s_up)
        share(b, spot)
        spot = place(2, 1)
        arrive(11, b, spot, whole)
        forward(19, b, spot, high, to_high, s_down)
        share(b, spot)
        for f, first in ((-1, 14), (1, 16)):
            spot = place(f, 2)
            arrive(first, b, spot, low)
            arrive(first + 1, b, spot, high)
            share(b, spot)

    def event4(b):
        spot = place(2, 2)
        arrive(18, b, spot, low)
        arrive(19, b, spot, high)
        share(b, spot)

    def event5(b):
        ref = gathered.at[:, :, 1 - c, :, span(b)]
        pltpu.make_async_remote_copy(
            src_ref=ref,
            dst_ref=ref,
            send_sem=own_sem,
            recv_sem=part_recv_sem.at[b],
            device_id=partner,
            device_id_type=MESH,
        ).wait_recv()

    def ring(slot, step, way):
        ref = tz.at[slot]
        return pltpu.make_async_remote_copy(
            src_ref=ref,
            dst_ref=ref,
            send_sem=z_send_sem.at[step, way],
            recv_sem=z_recv_sem.at[step, way],
            device_id=up if way == 0 else down,
            device_id_type=MESH,
        )

    locals_[0].wait()
    locals_[1].wait()
    tz[z, 0:8, :] = tgtv[q]
    tz[z, 8:16, :] = jnp.broadcast_to(wv[...], (8, structs))
    ring(z, 0, 0).start()
    ring(z, 0, 1).start()

    locals_[2].wait()
    ids = lax.broadcasted_iota(jnp.int32, (structs, atoms), 0)
    chosen = jnp.where(ids == segv[...], 1.0, 0.0).astype(F32)
    members[...] = chosen.T.astype(BF16)
    skt[...] = jnp.zeros_like(skt)
    locals_[6].wait()
    locals_[3].wait()

    def pivot_scales(k):
        at = pl.ds(pl.multiple_of(k * tile, tile), tile)
        total = jnp.zeros((tile, 128), F32)
        for j in range(pv.shape[1] // 128):
            part = pv[at, j * 128 : (j + 1) * 128].astype(F32)
            total = total + part * part
        scale = lax.rsqrt(jnp.sum(total, axis=1, keepdims=True) + EPS)
        squared = (desc_width * scale) * scale
        p2[at, :] = jnp.broadcast_to(squared, (tile, 128))

    desc_width = float(pv.shape[1])

    def atom_row(b):
        total = jnp.zeros((8, width), F32)
        for yi in range(NX):
            for xi in range(NX):
                part = gathered[yi, xi, :, :, span(b)].astype(F32)
                part = (part * part).reshape(2 * rows // 8, 8, width)
                total = total + jnp.sum(part, axis=0)
        arow[...] = lax.rsqrt(jnp.sum(total, axis=0, keepdims=True) + EPS)

    def compute(b, j):
        at = pl.ds(j * tile, tile)
        right = gathered[:, :, :, :, span(b)].reshape(pv.shape[1], width)
        scores = mm(pv[at, :], right)
        scaled = scores * arow[...]
        scaled = scaled * scaled
        factor = p2[at, :]
        factor = jnp.concatenate([factor] * (width // 128), axis=1)
        entries = (scaled * factor).astype(BF16)
        skt[at, :] += mm(entries, members[span(b), :])

    def step(k, carry):
        done = k - 4

        @pl.when(done >= 0)
        def _():
            event5(done)
            atom_row(done)

        stages = ((event4, 3), (event3, 2), (event2, 1), (event1, 0))
        for j, (event, lag) in enumerate(stages):

            @pl.when(jnp.logical_and(k >= lag, k < NB + lag))
            def _(event=event, lag=lag):
                event(k - lag)

            @pl.when(done >= 0)
            def _(j=j):
                compute(done, j)

        slot = lax.rem(z + NZ - 1 - k, NZ)
        ring(slot, k, 0).wait_recv()

        @pl.when(k < 7)
        def _():
            ring(slot, k + 1, 0).start()
            other = lax.rem(z + 1 + k, NZ)
            ring(other, k, 1).wait_recv()

            @pl.when(k < 6)
            def _():
                ring(other, k + 1, 1).start()

        @pl.when(k < 4)
        def _():
            pivot_scales(k)

        return carry

    lax.fori_loop(0, 8, step, 0)

    locals_[4].wait()
    coef_high, coef_low = split2(cv[...])
    sk_high, sk_low = split2(skt[...])
    n_targets = cv.shape[0]
    first = mm(jnp.concatenate([coef_high, coef_low], axis=0), sk_high)
    predicted = first[:n_targets] + first[n_targets:] + mm(coef_high, sk_low)
    pred_send[...] = predicted.reshape(n_targets // 8, 8, structs)
    pred_recv[p] = pred_send[q]

    def exchange(src_slot, dst_slot, peer):
        return pltpu.make_async_remote_copy(
            src_ref=pred_send.at[src_slot],
            dst_ref=pred_recv.at[dst_slot],
            send_sem=late_sem.at[0],
            recv_sem=late_sem.at[1],
            device_id=peer,
            device_id_type=MESH,
        )

    n_plane = pred_recv.shape[0]

    def send_tile(i, carry):
        peer = lax.rem(p + i, n_plane)
        exchange(lax.div(peer, 4), p, (z, peer)).start()
        return carry

    lax.fori_loop(1, n_plane, send_tile, 0)

    locals_[5].wait()
    wanted = destv[pl.ds(z, 1), :]
    home = jnp.zeros((48, structs), F32)
    for owner in range(NZ):
        spots = lax.broadcasted_iota(jnp.int32, (structs, structs), 0) + owner * structs
        pick = jnp.where(spots == wanted, 1.0, 0.0).astype(BF16)
        home = home + mm(jnp.concatenate(split3(tz[owner]), axis=0), pick)
    home = (home[0:16] + home[16:32]) + home[32:48]
    turned = skt[...].T
    sk_high, sk_low = split2(turned)
    sht[...] = sk_high
    slt[...] = sk_low

    def settle(ref, sem, sending):
        copy = pltpu.make_async_remote_copy(
            src_ref=ref,
            dst_ref=ref,
            send_sem=sem,
            recv_sem=sem,
            device_id=partner,
            device_id_type=MESH,
        )
        if sending:
            copy.wait_send()
        else:
            copy.wait_recv()

    settle(pred_recv.at[pl.ds(0, n_plane - 1)], late_sem.at[1], False)
    summed = jnp.sum(pred_recv[...], axis=0)
    resid = home[8:16] * (summed - home[0:8])
    tiles[q] = resid

    def tile_copy(yi, xi):
        return pltpu.make_async_remote_copy(
            src_ref=tiles.at[q],
            dst_ref=tiles.at[q],
            send_sem=late_sem.at[2],
            recv_sem=late_sem.at[3],
            device_id=(z, (yi * NX + xi) * 2 + c),
            device_id_type=MESH,
        )

    for dy in (2, 1, 3, 0):
        yi = lax.rem(y + dy, NX)
        tile_copy(yi, NX - 1 - x).start()
        if dy:
            tile_copy(yi, x).start()
    mine = lax.rem(p, 4)
    out = resid[0:2]
    for j in range(1, 4):
        out = jnp.where(mine == j, resid[2 * j : 2 * j + 2], out)
    res_ref[...] = out
    settle(tiles.at[pl.ds(0, 7)], late_sem.at[3], False)

    res_high, res_low = split2(tiles[...].reshape(n_targets, structs))
    first = mm(jnp.concatenate([res_high, res_low], axis=0), sht[...])
    grads = first[:n_targets] + first[n_targets:] + mm(res_high, slt[...])
    grads = grads * (1.0 / (structs * NZ))
    share_rows = n_targets // NZ
    for owner in range(NZ):
        grad_send[owner] = grads[owner * share_rows : (owner + 1) * share_rows]
    grad_recv[z] = grad_send[z]

    def send_grad(i, carry):
        peer = lax.rem(z + i, NZ)
        pltpu.make_async_remote_copy(
            src_ref=grad_send.at[peer],
            dst_ref=grad_recv.at[z],
            send_sem=late_sem.at[4],
            recv_sem=late_sem.at[5],
            device_id=(peer, p),
            device_id_type=MESH,
        ).start()
        return carry

    lax.fori_loop(1, NZ, send_grad, 0)

    settle(gathered.at[0, :, c], own_sem, True)
    settle(gathered.at[0:2, 0:3, c], line_sem, True)
    settle(gathered.at[0, 0, c], half_sem.at[0], True)
    settle(gathered.at[0, :, c], half_sem.at[1], True)
    settle(gathered.at[:, :, c], part_send_sem, True)
    for k in range(8):
        ring(z, k, 0).wait_send()
        if k < 7:
            ring(z, k, 1).wait_send()
    settle(pred_recv.at[pl.ds(0, n_plane - 1)], late_sem.at[0], True)
    settle(tiles.at[pl.ds(0, 7)], late_sem.at[2], True)
    settle(grad_recv.at[pl.ds(0, NZ - 1)], late_sem.at[5], False)
    grad_ref[...] = jnp.sum(grad_recv[...], axis=0)
    settle(grad_send.at[pl.ds(0, NZ - 1)], late_sem.at[4], True)


def on_device(descriptors, pivot_desc, coeffs, seg_ids, dest, targets, weights):
    atoms, rows = descriptors.shape
    pivots, width = pivot_desc.shape
    structs, n_targets = targets.shape
    any_spec = pl.BlockSpec(memory_space=pltpu.HBM)
    vmem_spec = pl.BlockSpec(memory_space=pltpu.VMEM)
    dma = pltpu.SemaphoreType.DMA
    res, grad = pl.pallas_call(
        kernel,
        out_shape=(
            jax.ShapeDtypeStruct((n_targets // 32, structs), F32),
            jax.ShapeDtypeStruct((n_targets // NZ, pivots), F32),
        ),
        in_specs=[any_spec] * 7,
        out_specs=(vmem_spec, vmem_spec),
        scratch_shapes=[
            pltpu.VMEM((NX, NX, 2, rows, atoms), BF16),
            pltpu.VMEM((pivots, width), BF16),
            pltpu.VMEM((n_targets, pivots), F32),
            pltpu.VMEM((1, atoms), jnp.int32),
            pltpu.VMEM((NZ, structs), jnp.int32),
            pltpu.VMEM((n_targets // 8, 8, structs), F32),
            pltpu.VMEM((1, structs), F32),
            pltpu.VMEM((pivots, 128), F32),
            pltpu.VMEM((atoms, structs), BF16),
            pltpu.VMEM((pivots, structs), F32),
            pltpu.VMEM((structs, pivots), BF16),
            pltpu.VMEM((structs, pivots), BF16),
            pltpu.VMEM((NZ, 16, structs), F32),
            pltpu.VMEM((n_targets // 8, 8, structs), F32),
            pltpu.VMEM((32, 8, structs), F32),
            pltpu.VMEM((n_targets // 8, 8, structs), F32),
            pltpu.VMEM((NZ, n_targets // NZ, pivots), F32),
            pltpu.VMEM((NZ, n_targets // NZ, pivots), F32),
            pltpu.VMEM((1, atoms // NB), F32),
            dma((7,)),
            dma,
            dma,
            dma((2,)),
            dma,
            dma((20, NB)),
            dma((NB,)),
            dma((8, 2)),
            dma((8, 2)),
            dma((6,)),
        ],
        compiler_params=pltpu.CompilerParams(
            collective_id=0, has_side_effects=True, vmem_limit_bytes=60 * 1024 * 1024
        ),
        name="fit_gradient",
    )(
        descriptors.T,
        pivot_desc,
        coeffs.T,
        seg_ids,
        dest.reshape(NZ, structs),
        targets.T.reshape(n_targets // 8, 8, structs),
        weights.reshape(1, structs),
    )
    return res.T, grad


def solution(mesh):
    placed = (
        P("atoms", "pivots"),
        P("pivots", None),
        P("pivots", None),
        P("atoms", None),
        P(),
        P("atoms", None),
        P("atoms"),
    )
    return jax.shard_map(
        on_device,
        mesh=mesh,
        in_specs=placed,
        out_specs=(P("atoms", "pivots"), P("atoms", "pivots")),
        check_vma=False,
    )
```

```python
import functools

import jax
import jax.numpy as jnp
from jax import lax
from jax.experimental import pallas as pl
from jax.experimental.pallas import tpu as pltpu
from jax.sharding import PartitionSpec as P

EPS = 1e-6
MESH = pl.DeviceIdType.MESH
F32 = jnp.float32
BF16 = jnp.bfloat16
CODES = 32766.0
NB = 2
NZ = 16
NX = 4


def split2(value):
    high = value.astype(BF16)
    low = (value - high.astype(F32)).astype(BF16)
    return high, low


def split3(value):
    high = value.astype(BF16)
    rest = value - high.astype(F32)
    mid = rest.astype(BF16)
    low = (rest - mid.astype(F32)).astype(BF16)
    return high, mid, low


def mm(left, right):
    return jnp.dot(left, right, preferred_element_type=F32)


def kernel(
    d_ref,
    p_ref,
    c_ref,
    seg_ref,
    dest_ref,
    tgt_ref,
    w_ref,
    res_ref,
    grad_ref,
    gathered,
    pv,
    cv,
    segv,
    destv,
    tgtv,
    wv,
    p2,
    members,
    skt,
    sht,
    slt,
    tz,
    pred_send,
    pred_recv,
    tiles,
    grad_send,
    grad_recv,
    step_send,
    step_recv,
    squares,
    scores,
    local_sem,
    own_sem,
    line_sem,
    half_sem,
    part_send_sem,
    recv_sem,
    part_recv_sem,
    known_sem,
    late_sem,
):
    z = lax.axis_index("atoms")
    p = lax.axis_index("pivots")
    c = lax.rem(p, 2)
    x = lax.rem(lax.div(p, 2), NX)
    y = lax.div(p, 2 * NX)
    q = lax.div(p, 4)
    rows = d_ref.shape[0]
    half = rows // 2
    atoms = d_ref.shape[1]
    width = atoms // NB
    pivots = p_ref.shape[0]
    tile = pivots // 4
    structs = tz.shape[2]

    def wrap(value):
        return lax.rem(value + NX, NX)

    def place(f, s):
        return wrap(y + s * (1 - c) + f * c), wrap(x + f * (1 - c) + s * c)

    def device(f, s):
        yi, xi = place(f, s)
        return (z, (yi * NX + xi) * 2 + c)

    partner = (z, p + 1 - 2 * c)
    up = (lax.rem(z + 1, NZ), p)
    down = (lax.rem(z + NZ - 1, NZ), p)
    f_up, f_down = device(1, 0), device(-1, 0)
    s_up, s_down = device(0, 1), device(0, -1)

    locals_ = [
        pltpu.make_async_copy(tgt_ref, tgtv, local_sem.at[0]),
        pltpu.make_async_copy(w_ref, wv, local_sem.at[1]),
        pltpu.make_async_copy(seg_ref, segv, local_sem.at[2]),
        pltpu.make_async_copy(p_ref, pv, local_sem.at[3]),
        pltpu.make_async_copy(c_ref, cv, local_sem.at[4]),
        pltpu.make_async_copy(dest_ref, destv, local_sem.at[5]),
        pltpu.make_async_copy(d_ref, gathered.at[y, x, c], local_sem.at[6]),
    ]
    barrier = pltpu.get_barrier_semaphore()
    for peer in (f_up, f_down, s_up, s_down, partner, up, down):
        pl.semaphore_signal(barrier, inc=1, device_id=peer, device_id_type=MESH)
    for copy in locals_:
        copy.start()
    pl.semaphore_wait(barrier, 7)

    def span(b):
        return pl.ds(pl.multiple_of(b * width, width), width)

    def own(b):
        for kind, peer in ((0, f_up), (1, f_down), (2, s_up), (3, s_down)):
            pltpu.make_async_remote_copy(
                src_ref=d_ref.at[:, span(b)],
                dst_ref=gathered.at[y, x, c, :, span(b)],
                send_sem=own_sem,
                recv_sem=recv_sem.at[kind, b],
                device_id=peer,
                device_id_type=MESH,
            ).start()
        pltpu.make_async_remote_copy(
            src_ref=d_ref.at[:, span(b)],
            dst_ref=gathered.at[y, x, c, :, span(b)],
            send_sem=part_send_sem,
            recv_sem=part_recv_sem.at[0],
            device_id=partner,
            device_id_type=MESH,
        ).start()

    for b in range(NB):
        own(b)

    def piece(spot, part, b):
        yi, xi = spot
        return gathered.at[yi, xi, c, part, span(b)]

    whole, low, high = pl.ds(0, rows), pl.ds(0, half), pl.ds(half, half)

    def forward(kind, b, spot, part, sem, peer):
        ref = piece(spot, part, b)
        pltpu.make_async_remote_copy(
            src_ref=ref,
            dst_ref=ref,
            send_sem=sem,
            recv_sem=recv_sem.at[kind, b],
            device_id=peer,
            device_id_type=MESH,
        ).start()

    def share(b, spot, group):
        ref = piece(spot, whole, b)
        pltpu.make_async_remote_copy(
            src_ref=ref,
            dst_ref=ref,
            send_sem=part_send_sem,
            recv_sem=part_recv_sem.at[group],
            device_id=partner,
            device_id_type=MESH,
        ).start()

    def arrive(kind, b, spot, part):
        ref = piece(spot, part, b)
        pltpu.make_async_remote_copy(
            src_ref=ref,
            dst_ref=ref,
            send_sem=own_sem,
            recv_sem=recv_sem.at[kind, b],
            device_id=partner,
            device_id_type=MESH,
        ).wait_recv()

    to_low, to_high = half_sem.at[0], half_sem.at[1]

    def event1(b):
        spot = place(-1, 0)
        arrive(0, b, spot, whole)
        forward(4, b, spot, low, to_low, f_up)
        forward(6, b, spot, whole, line_sem, s_up)
        forward(7, b, spot, whole, line_sem, s_down)
        share(b, spot, 1)
        spot = place(1, 0)
        arrive(1, b, spot, whole)
        forward(5, b, spot, high, to_low, f_down)
        forward(8, b, spot, whole, line_sem, s_up)
        forward(9, b, spot, whole, line_sem, s_down)
        share(b, spot, 1)
        spot = place(0, -1)
        arrive(2, b, spot, whole)
        forward(12, b, spot, low, to_high, s_up)
        share(b, spot, 1)
        spot = place(0, 1)
        arrive(3, b, spot, whole)
        forward(13, b, spot, high, to_high, s_down)
        share(b, spot, 1)

    def event2(b):
        spot = place(2, 0)
        arrive(4, b, spot, low)
        arrive(5, b, spot, high)
        forward(10, b, spot, whole, line_sem, s_up)
        forward(11, b, spot, whole, line_sem, s_down)
        share(b, spot, 2)
        for f, first in ((-1, 6), (1, 8)):
            spot = place(f, -1)
            arrive(first, b, spot, whole)
            forward(first + 8, b, spot, low, to_high, s_up)
            share(b, spot, 2)
            spot = place(f, 1)
            arrive(first + 1, b, spot, whole)
            forward(first + 9, b, spot, high, to_high, s_down)
            share(b, spot, 2)
        spot = place(0, 2)
        arrive(12, b, spot, low)
        arrive(13, b, spot, high)
        share(b, spot, 2)

    def event3(b):
        spot = place(2, -1)
        arrive(10, b, spot, whole)
        forward(18, b, spot, low, to_high, s_up)
        share(b, spot, 3)
        spot = place(2, 1)
        arrive(11, b, spot, whole)
        forward(19, b, spot, high, to_high, s_down)
        share(b, spot, 3)
        for f, first in ((-1, 14), (1, 16)):
            spot = place(f, 2)
            arrive(first, b, spot, low)
            arrive(first + 1, b, spot, high)
            share(b, spot, 3)

    def event4(b):
        spot = place(2, 2)
        arrive(18, b, spot, low)
        arrive(19, b, spot, high)
        share(b, spot, 4)

    def shared(ref, group):
        pltpu.make_async_remote_copy(
            src_ref=ref,
            dst_ref=ref,
            send_sem=own_sem,
            recv_sem=part_recv_sem.at[group],
            device_id=partner,
            device_id_type=MESH,
        ).wait_recv()

    def greet(distance, step):
        for peer in (lax.rem(z + distance, NZ), lax.rem(z + NZ - distance, NZ)):
            pl.semaphore_signal(known_sem.at[step], inc=1, device_id=(peer, p), device_id_type=MESH)

    greet(1, 0)

    locals_[0].wait()
    locals_[1].wait()
    tz[z, 0:8, :] = tgtv[q]
    tz[z, 8:16, :] = jnp.broadcast_to(wv[...], (8, structs))

    locals_[2].wait()
    ids = lax.broadcasted_iota(jnp.int32, (structs, atoms), 0)
    chosen = jnp.where(ids == segv[...], 1.0, 0.0).astype(F32)
    members[...] = chosen.T.astype(BF16)
    locals_[6].wait()
    locals_[3].wait()

    def pivot_scales(k):
        at = pl.ds(pl.multiple_of(k * tile, tile), tile)
        total = jnp.zeros((tile, 128), F32)
        for j in range(pv.shape[1] // 128):
            part = pv[at, j * 128 : (j + 1) * 128].astype(F32)
            total = total + part * part
        scale = lax.rsqrt(jnp.sum(total, axis=1, keepdims=True) + EPS)
        squared = (desc_width * scale) * scale
        p2[at, :] = jnp.broadcast_to(squared, (tile, 128))

    desc_width = float(pv.shape[1])

    def chip(dy, dx):
        return wrap(y + dy), wrap(x + dx)

    def operand(chips):
        parts = [gathered[yi, xi].reshape(2 * rows, atoms) for yi, xi in chips]
        return jnp.concatenate(parts, axis=0)

    def columns(at, chips):
        parts = []
        for yi, xi in chips:
            first = pl.multiple_of((yi * NX + xi) * 2 * rows, 128)
            parts.append(pv[at, pl.ds(first, 2 * rows)])
        return jnp.concatenate(parts, axis=1)

    def add_squares(chips, start):
        total = jnp.zeros((8, atoms), F32) if start else squares[...]
        for yi, xi in chips:
            part = gathered[yi, xi].astype(F32)
            part = (part * part).reshape(2 * rows // 8, 8, atoms)
            total = total + jnp.sum(part, axis=0)
        squares[...] = total

    def add_scores(chips, start):
        right = operand(chips)
        for j in range(pivots // tile):
            at = pl.ds(j * tile, tile)
            part = mm(columns(at, chips), right)
            scores[at, :] = part if start else scores[at, :] + part
        add_squares(chips, start)

    def finish(chips):
        add_squares(chips, False)
        row = lax.rsqrt(jnp.sum(squares[...], axis=0, keepdims=True) + EPS)
        right = operand(chips)
        for j in range(pivots // tile):
            at = pl.ds(j * tile, tile)
            scaled = (scores[at, :] + mm(columns(at, chips), right)) * row
            scaled = scaled * scaled
            factor = jnp.concatenate([p2[at, :]] * (atoms // 128), axis=1)
            entries = (scaled * factor).astype(BF16)
            skt[at, :] = mm(entries, members[...])

    def settle(ref, sem, sending):
        copy = pltpu.make_async_remote_copy(
            src_ref=ref,
            dst_ref=ref,
            send_sem=sem,
            recv_sem=sem,
            device_id=partner,
            device_id_type=MESH,
        )
        if sending:
            copy.wait_send()
        else:
            copy.wait_recv()

    def send_owner(i):
        pltpu.make_async_remote_copy(
            src_ref=tz.at[z],
            dst_ref=tz.at[z],
            send_sem=late_sem.at[8],
            recv_sem=late_sem.at[9],
            device_id=(lax.rem(z + i, NZ), p),
            device_id_type=MESH,
        ).start()

    event1(0)
    pl.semaphore_wait(known_sem.at[0], 2)
    greet(2, 1)
    for b in range(1, NB):
        event1(b)
    for k in range(pivots // tile):
        pivot_scales(k)
    pl.semaphore_wait(known_sem.at[1], 2)
    greet(4, 2)
    shared(gathered.at[0, :, c], 1)
    add_scores([chip(0, -1), chip(0, 1), chip(-1, 0), chip(1, 0)], True)
    for b in range(NB):
        event2(b)
    pl.semaphore_wait(known_sem.at[2], 2)
    for i in (8, 7, 9, 6, 10, 5, 11, 4, 12, 3, 13, 2, 14, 1, 15):
        send_owner(i)
    shared(gathered.at[0, 0, c], 0)
    shared(gathered.at[0:2, 0:3, c], 2)
    add_scores([chip(0, 0), chip(0, 2), chip(-1, -1), chip(-1, 1), chip(1, -1), chip(1, 1)], False)
    for b in range(NB):
        event3(b)
    shared(gathered.at[0, :, c], 3)
    add_scores([chip(2, 0), chip(1, 2), chip(-1, 2), chip(2, -1)], False)
    for b in range(NB):
        event4(b)
    shared(gathered.at[0, 0, c], 4)
    finish([chip(2, 1), chip(2, 2)])

    locals_[4].wait()
    coef_high, coef_low = split2(cv[...])
    sk_high, sk_low = split2(skt[...])
    n_targets = cv.shape[0]
    first = mm(jnp.concatenate([coef_high, coef_low], axis=0), sk_high)
    predicted = first[:n_targets] + first[n_targets:] + mm(coef_high, sk_low)
    pred_send[...] = predicted.reshape(n_targets // 8, 8, structs)
    pred_recv[p] = pred_send[q]

    def exchange(src_slot, dst_slot, peer):
        return pltpu.make_async_remote_copy(
            src_ref=pred_send.at[src_slot],
            dst_ref=pred_recv.at[dst_slot],
            send_sem=late_sem.at[0],
            recv_sem=late_sem.at[1],
            device_id=peer,
            device_id_type=MESH,
        )

    n_plane = pred_recv.shape[0]

    far = sorted(range(1, n_plane), key=lambda i: -sum(min(v, NX - v) for v in (i // 2 // NX, i // 2 % NX)))
    for i in far:
        yi, xi = chip(i // 2 // NX, i // 2 % NX)
        peer = (yi * NX + xi) * 2 + (c if i % 2 == 0 else 1 - c)
        exchange(lax.div(peer, 4), p, (z, peer)).start()

    locals_[5].wait()
    settle(tz.at[pl.ds(0, NZ - 1)], late_sem.at[9], False)
    wanted = destv[pl.ds(z, 1), :]
    home = jnp.zeros((48, structs), F32)
    for owner in range(NZ):
        spots = lax.broadcasted_iota(jnp.int32, (structs, structs), 0) + owner * structs
        pick = jnp.where(spots == wanted, 1.0, 0.0).astype(BF16)
        home = home + mm(jnp.concatenate(split3(tz[owner]), axis=0), pick)
    home = (home[0:16] + home[16:32]) + home[32:48]
    turned = skt[...].T
    sk_high, sk_low = split2(turned)
    sht[...] = sk_high
    slt[...] = sk_low

    settle(pred_recv.at[pl.ds(0, n_plane - 1)], late_sem.at[1], False)
    summed = jnp.sum(pred_recv[...], axis=0)
    resid = home[8:16] * (summed - home[0:8])
    tiles[q] = resid

    def tile_copy(yi, xi):
        return pltpu.make_async_remote_copy(
            src_ref=tiles.at[q],
            dst_ref=tiles.at[q],
            send_sem=late_sem.at[2],
            recv_sem=late_sem.at[3],
            device_id=(z, (yi * NX + xi) * 2 + c),
            device_id_type=MESH,
        )

    for dy in (2, 1, 3, 0):
        yi = lax.rem(y + dy, NX)
        tile_copy(yi, NX - 1 - x).start()
        if dy:
            tile_copy(yi, x).start()
    mine = lax.rem(p, 4)
    out = resid[0:2]
    for j in range(1, 4):
        out = jnp.where(mine == j, resid[2 * j : 2 * j + 2], out)
    res_ref[...] = out
    settle(tiles.at[pl.ds(0, 7)], late_sem.at[3], False)

    res_high, res_low = split2(tiles[...].reshape(n_targets, structs))
    first = mm(jnp.concatenate([res_high, res_low], axis=0), sht[...])
    grads = first[:n_targets] + first[n_targets:] + mm(res_high, slt[...])
    grads = grads * (1.0 / (structs * NZ))
    share_rows = n_targets // NZ
    largest = jnp.max(jnp.max(jnp.abs(grads), axis=0, keepdims=True), axis=1, keepdims=True)
    largest = jnp.maximum(jnp.broadcast_to(largest, (1, 128)), 1e-30)
    step_send[...] = largest * (1.0 / CODES)
    to_code = jnp.broadcast_to(CODES / largest, (n_targets, 128))
    to_code = jnp.concatenate([to_code] * (pivots // 128), axis=1)
    codes = jnp.floor(grads * to_code + 0.5).astype(jnp.int32)
    for owner in range(NZ):
        part = codes[owner * share_rows : (owner + 1) * share_rows]
        part = jnp.concatenate([part[:, k * 256 : (k + 1) * 256] for k in range(pivots // 256)], axis=0)
        grad_send[owner] = part.astype(jnp.int16)
    grad_recv[z] = grad_send[z]
    step_recv[z] = step_send[...]

    def send_grad(i, carry):
        peer = lax.rem(z + i, NZ)
        for src, dst, sem in (
            (grad_send.at[peer], grad_recv.at[z], 4),
            (step_send, step_recv.at[z], 6),
        ):
            pltpu.make_async_remote_copy(
                src_ref=src,
                dst_ref=dst,
                send_sem=late_sem.at[sem],
                recv_sem=late_sem.at[sem + 1],
                device_id=(peer, p),
                device_id_type=MESH,
            ).start()
        return carry

    for i in (8, 7, 9, 6, 10, 5, 11, 4, 12, 3, 13, 2, 14, 1, 15):
        send_grad(i, 0)

    settle(gathered.at[0, :, c], own_sem, True)
    settle(gathered.at[0:2, 0:3, c], line_sem, True)
    settle(gathered.at[0, 0, c], half_sem.at[0], True)
    settle(gathered.at[0, :, c], half_sem.at[1], True)
    settle(gathered.at[:, :, c], part_send_sem, True)
    settle(tz.at[pl.ds(0, NZ - 1)], late_sem.at[8], True)
    settle(pred_recv.at[pl.ds(0, n_plane - 1)], late_sem.at[0], True)
    settle(tiles.at[pl.ds(0, 7)], late_sem.at[2], True)
    settle(grad_recv.at[pl.ds(0, NZ - 1)], late_sem.at[5], False)
    settle(step_recv.at[pl.ds(0, NZ - 1)], late_sem.at[7], False)
    settle(step_recv.at[pl.ds(0, NZ - 1)], late_sem.at[6], True)
    total = jnp.zeros(grad_recv.shape[1:], F32)
    for src in range(NZ):
        scale = step_recv[src]
        scale = jnp.concatenate([scale, scale], axis=1)
        total = total + grad_recv[src].astype(jnp.int32).astype(F32) * scale
    for k in range(pivots // 256):
        grad_ref[:, k * 256 : (k + 1) * 256] = total[k * share_rows : (k + 1) * share_rows]
    settle(grad_send.at[pl.ds(0, NZ - 1)], late_sem.at[4], True)


def on_device(descriptors, pivot_desc, coeffs, seg_ids, dest, targets, weights):
    atoms, rows = descriptors.shape
    pivots, width = pivot_desc.shape
    structs, n_targets = targets.shape
    any_spec = pl.BlockSpec(memory_space=pltpu.HBM)
    vmem_spec = pl.BlockSpec(memory_space=pltpu.VMEM)
    dma = pltpu.SemaphoreType.DMA
    res, grad = pl.pallas_call(
        kernel,
        out_shape=(
            jax.ShapeDtypeStruct((n_targets // 32, structs), F32),
            jax.ShapeDtypeStruct((n_targets // NZ, pivots), F32),
        ),
        in_specs=[any_spec] * 7,
        out_specs=(vmem_spec, vmem_spec),
        scratch_shapes=[
            pltpu.VMEM((NX, NX, 2, rows, atoms), BF16),
            pltpu.VMEM((pivots, width), BF16),
            pltpu.VMEM((n_targets, pivots), F32),
            pltpu.VMEM((1, atoms), jnp.int32),
            pltpu.VMEM((NZ, structs), jnp.int32),
            pltpu.VMEM((n_targets // 8, 8, structs), F32),
            pltpu.VMEM((1, structs), F32),
            pltpu.VMEM((pivots, 128), F32),
            pltpu.VMEM((atoms, structs), BF16),
            pltpu.VMEM((pivots, structs), F32),
            pltpu.VMEM((structs, pivots), BF16),
            pltpu.VMEM((structs, pivots), BF16),
            pltpu.VMEM((NZ, 16, structs), F32),
            pltpu.VMEM((n_targets // 8, 8, structs), F32),
            pltpu.VMEM((32, 8, structs), F32),
            pltpu.VMEM((n_targets // 8, 8, structs), F32),
            pltpu.VMEM((NZ, 16, 256), jnp.int16),
            pltpu.VMEM((NZ, 16, 256), jnp.int16),
            pltpu.VMEM((1, 128), F32),
            pltpu.VMEM((NZ, 1, 128), F32),
            pltpu.VMEM((8, atoms), F32),
            pltpu.VMEM((pivots, atoms), F32),
            dma((7,)),
            dma,
            dma,
            dma((2,)),
            dma,
            dma((20, NB)),
            dma((5,)),
            pltpu.SemaphoreType.REGULAR((3,)),
            dma((10,)),
        ],
        compiler_params=pltpu.CompilerParams(
            collective_id=0, has_side_effects=True, vmem_limit_bytes=60 * 1024 * 1024
        ),
        name="fit_gradient",
    )(
        descriptors.T,
        pivot_desc,
        coeffs.T,
        seg_ids,
        dest.reshape(NZ, structs),
        targets.T.reshape(n_targets // 8, 8, structs),
        weights.reshape(1, structs),
    )
    return res.T, grad


def solution(mesh):
    placed = (
        P("atoms", "pivots"),
        P("pivots", None),
        P("pivots", None),
        P("atoms", None),
        P(),
        P("atoms", None),
        P("atoms"),
    )
    return jax.shard_map(
        on_device,
        mesh=mesh,
        in_specs=placed,
        out_specs=(P("atoms", "pivots"), P("atoms", "pivots")),
        check_vma=False,
    )
```

```python
import functools

import jax
import jax.numpy as jnp
from jax import lax
from jax.experimental import pallas as pl
from jax.experimental.pallas import tpu as pltpu
from jax.sharding import PartitionSpec as P

EPS = 1e-6
MESH = pl.DeviceIdType.MESH
F32 = jnp.float32
BF16 = jnp.bfloat16
CODES = 32766.0
NB = 2
NZ = 16
NX = 4


def split2(value):
    high = value.astype(BF16)
    low = (value - high.astype(F32)).astype(BF16)
    return high, low


def split3(value):
    high = value.astype(BF16)
    rest = value - high.astype(F32)
    mid = rest.astype(BF16)
    low = (rest - mid.astype(F32)).astype(BF16)
    return high, mid, low


def mm(left, right):
    return jnp.dot(left, right, preferred_element_type=F32)


def kernel(
    d_ref,
    p_ref,
    c_ref,
    seg_ref,
    dest_ref,
    tgt_ref,
    w_ref,
    res_ref,
    grad_ref,
    gathered,
    pv,
    cv,
    segv,
    destv,
    tgtv,
    wv,
    p2,
    members,
    skt,
    sht,
    slt,
    tz,
    pred_send,
    pred_recv,
    tiles,
    grad_send,
    grad_recv,
    step_send,
    step_recv,
    squares,
    scores,
    local_sem,
    own_sem,
    line_sem,
    half_sem,
    part_send_sem,
    recv_sem,
    part_recv_sem,
    known_sem,
    late_sem,
):
    z = lax.axis_index("atoms")
    p = lax.axis_index("pivots")
    c = lax.rem(p, 2)
    x = lax.rem(lax.div(p, 2), NX)
    y = lax.div(p, 2 * NX)
    q = lax.div(p, 4)
    rows = d_ref.shape[0]
    half = rows // 2
    atoms = d_ref.shape[1]
    width = atoms // NB
    pivots = p_ref.shape[0]
    tile = pivots // 4
    structs = tz.shape[2]

    def wrap(value):
        return lax.rem(value + NX, NX)

    def place(f, s):
        return wrap(y + s * (1 - c) + f * c), wrap(x + f * (1 - c) + s * c)

    def device(f, s):
        yi, xi = place(f, s)
        return (z, (yi * NX + xi) * 2 + c)

    partner = (z, p + 1 - 2 * c)
    up = (lax.rem(z + 1, NZ), p)
    down = (lax.rem(z + NZ - 1, NZ), p)
    f_up, f_down = device(1, 0), device(-1, 0)
    s_up, s_down = device(0, 1), device(0, -1)

    locals_ = [
        pltpu.make_async_copy(tgt_ref, tgtv, local_sem.at[0]),
        pltpu.make_async_copy(w_ref, wv, local_sem.at[1]),
        pltpu.make_async_copy(seg_ref, segv, local_sem.at[2]),
        pltpu.make_async_copy(p_ref, pv, local_sem.at[3]),
        pltpu.make_async_copy(c_ref, cv, local_sem.at[4]),
        pltpu.make_async_copy(dest_ref, destv, local_sem.at[5]),
        pltpu.make_async_copy(d_ref, gathered.at[y, x, c], local_sem.at[6]),
    ]
    barrier = pltpu.get_barrier_semaphore()
    for peer in (f_up, f_down, s_up, s_down, partner, up, down):
        pl.semaphore_signal(barrier, inc=1, device_id=peer, device_id_type=MESH)
    locals_[6].start()
    for k in (0, 1, 2):
        locals_[k].start()
    pl.semaphore_wait(barrier, 7)

    def span(b):
        return pl.ds(pl.multiple_of(b * width, width), width)

    def own(b):
        for kind, peer in ((0, f_up), (1, f_down), (2, s_up), (3, s_down)):
            pltpu.make_async_remote_copy(
                src_ref=gathered.at[y, x, c, :, span(b)],
                dst_ref=gathered.at[y, x, c, :, span(b)],
                send_sem=own_sem,
                recv_sem=recv_sem.at[kind, b],
                device_id=peer,
                device_id_type=MESH,
            ).start()
        pltpu.make_async_remote_copy(
            src_ref=gathered.at[y, x, c, :, span(b)],
            dst_ref=gathered.at[y, x, c, :, span(b)],
            send_sem=part_send_sem,
            recv_sem=part_recv_sem.at[0],
            device_id=partner,
            device_id_type=MESH,
        ).start()

    locals_[6].wait()
    for b in range(NB):
        own(b)
    for k in (3, 4, 5):
        locals_[k].start()

    def piece(spot, part, b):
        yi, xi = spot
        return gathered.at[yi, xi, c, part, span(b)]

    whole, low, high = pl.ds(0, rows), pl.ds(0, half), pl.ds(half, half)

    def forward(kind, b, spot, part, sem, peer):
        ref = piece(spot, part, b)
        pltpu.make_async_remote_copy(
            src_ref=ref,
            dst_ref=ref,
            send_sem=sem,
            recv_sem=recv_sem.at[kind, b],
            device_id=peer,
            device_id_type=MESH,
        ).start()

    def share(b, spot, group):
        ref = piece(spot, whole, b)
        pltpu.make_async_remote_copy(
            src_ref=ref,
            dst_ref=ref,
            send_sem=part_send_sem,
            recv_sem=part_recv_sem.at[group],
            device_id=partner,
            device_id_type=MESH,
        ).start()

    def arrive(kind, b, spot, part):
        ref = piece(spot, part, b)
        pltpu.make_async_remote_copy(
            src_ref=ref,
            dst_ref=ref,
            send_sem=own_sem,
            recv_sem=recv_sem.at[kind, b],
            device_id=partner,
            device_id_type=MESH,
        ).wait_recv()

    to_low, to_high = half_sem.at[0], half_sem.at[1]

    def event1(b):
        spot = place(-1, 0)
        arrive(0, b, spot, whole)
        forward(4, b, spot, low, to_low, f_up)
        forward(6, b, spot, whole, line_sem, s_up)
        forward(7, b, spot, whole, line_sem, s_down)
        share(b, spot, 1)
        spot = place(1, 0)
        arrive(1, b, spot, whole)
        forward(5, b, spot, high, to_low, f_down)
        forward(8, b, spot, whole, line_sem, s_up)
        forward(9, b, spot, whole, line_sem, s_down)
        share(b, spot, 1)
        spot = place(0, -1)
        arrive(2, b, spot, whole)
        forward(12, b, spot, low, to_high, s_up)
        share(b, spot, 1)
        spot = place(0, 1)
        arrive(3, b, spot, whole)
        forward(13, b, spot, high, to_high, s_down)
        share(b, spot, 1)

    def event2(b):
        spot = place(2, 0)
        arrive(4, b, spot, low)
        arrive(5, b, spot, high)
        forward(10, b, spot, whole, line_sem, s_up)
        forward(11, b, spot, whole, line_sem, s_down)
        share(b, spot, 2)
        for f, first in ((-1, 6), (1, 8)):
            spot = place(f, -1)
            arrive(first, b, spot, whole)
            forward(first + 8, b, spot, low, to_high, s_up)
            share(b, spot, 2)
            spot = place(f, 1)
            arrive(first + 1, b, spot, whole)
            forward(first + 9, b, spot, high, to_high, s_down)
            share(b, spot, 2)
        spot = place(0, 2)
        arrive(12, b, spot, low)
        arrive(13, b, spot, high)
        share(b, spot, 2)

    def event3(b):
        spot = place(2, -1)
        arrive(10, b, spot, whole)
        forward(18, b, spot, low, to_high, s_up)
        share(b, spot, 3)
        spot = place(2, 1)
        arrive(11, b, spot, whole)
        forward(19, b, spot, high, to_high, s_down)
        share(b, spot, 3)
        for f, first in ((-1, 14), (1, 16)):
            spot = place(f, 2)
            arrive(first, b, spot, low)
            arrive(first + 1, b, spot, high)
            share(b, spot, 3)

    def event4(b):
        spot = place(2, 2)
        arrive(18, b, spot, low)
        arrive(19, b, spot, high)
        share(b, spot, 4)

    def shared(ref, group):
        pltpu.make_async_remote_copy(
            src_ref=ref,
            dst_ref=ref,
            send_sem=own_sem,
            recv_sem=part_recv_sem.at[group],
            device_id=partner,
            device_id_type=MESH,
        ).wait_recv()

    def greet(distance, step):
        for peer in (lax.rem(z + distance, NZ), lax.rem(z + NZ - distance, NZ)):
            pl.semaphore_signal(known_sem.at[step], inc=1, device_id=(peer, p), device_id_type=MESH)

    greet(1, 0)

    locals_[0].wait()
    locals_[1].wait()
    tz[z, 0:8, :] = tgtv[q]
    tz[z, 8:16, :] = jnp.broadcast_to(wv[...], (8, structs))

    locals_[2].wait()
    ids = lax.broadcasted_iota(jnp.int32, (structs, atoms), 0)
    chosen = jnp.where(ids == segv[...], 1.0, 0.0).astype(F32)
    members[...] = chosen.T.astype(BF16)

    def pivot_scales(k):
        at = pl.ds(pl.multiple_of(k * tile, tile), tile)
        total = jnp.zeros((tile, 128), F32)
        for j in range(pv.shape[1] // 128):
            part = pv[at, j * 128 : (j + 1) * 128].astype(F32)
            total = total + part * part
        scale = lax.rsqrt(jnp.sum(total, axis=1, keepdims=True) + EPS)
        squared = (desc_width * scale) * scale
        p2[at, :] = jnp.broadcast_to(squared, (tile, 128))

    desc_width = float(pv.shape[1])

    def chip(dy, dx):
        return wrap(y + dy), wrap(x + dx)

    def operand(chips):
        parts = [gathered[yi, xi].reshape(2 * rows, atoms) for yi, xi in chips]
        return jnp.concatenate(parts, axis=0)

    def columns(at, chips):
        parts = []
        for yi, xi in chips:
            first = pl.multiple_of((yi * NX + xi) * 2 * rows, 128)
            parts.append(pv[at, pl.ds(first, 2 * rows)])
        return jnp.concatenate(parts, axis=1)

    def add_squares(chips, start):
        total = jnp.zeros((8, atoms), F32) if start else squares[...]
        for yi, xi in chips:
            part = gathered[yi, xi].astype(F32)
            part = (part * part).reshape(2 * rows // 8, 8, atoms)
            total = total + jnp.sum(part, axis=0)
        squares[...] = total

    def add_scores(chips, start):
        right = operand(chips)
        for j in range(pivots // tile):
            at = pl.ds(j * tile, tile)
            part = mm(columns(at, chips), right)
            scores[at, :] = part if start else scores[at, :] + part
        add_squares(chips, start)

    def finish(chips):
        add_squares(chips, False)
        row = lax.rsqrt(jnp.sum(squares[...], axis=0, keepdims=True) + EPS)
        right = operand(chips)
        for j in range(pivots // tile):
            at = pl.ds(j * tile, tile)
            scaled = (scores[at, :] + mm(columns(at, chips), right)) * row
            scaled = scaled * scaled
            factor = jnp.concatenate([p2[at, :]] * (atoms // 128), axis=1)
            entries = (scaled * factor).astype(BF16)
            skt[at, :] = mm(entries, members[...])

    def settle(ref, sem, sending):
        copy = pltpu.make_async_remote_copy(
            src_ref=ref,
            dst_ref=ref,
            send_sem=sem,
            recv_sem=sem,
            device_id=partner,
            device_id_type=MESH,
        )
        if sending:
            copy.wait_send()
        else:
            copy.wait_recv()

    def send_owner(i):
        pltpu.make_async_remote_copy(
            src_ref=tz.at[z],
            dst_ref=tz.at[z],
            send_sem=late_sem.at[8],
            recv_sem=late_sem.at[9],
            device_id=(lax.rem(z + i, NZ), p),
            device_id_type=MESH,
        ).start()

    locals_[3].wait()
    for k in range(pivots // tile):
        pivot_scales(k)
    event1(0)
    pl.semaphore_wait(known_sem.at[0], 2)
    greet(2, 1)
    event1(1)
    pl.semaphore_wait(known_sem.at[1], 2)
    greet(4, 2)
    event2(0)
    event2(1)
    pl.semaphore_wait(known_sem.at[2], 2)
    for i in (8, 7, 9, 6, 10, 5, 11, 4, 12, 3, 13, 2, 14, 1, 15):
        send_owner(i)
    shared(gathered.at[0, :, c], 1)
    add_scores([chip(0, -1), chip(0, 1), chip(-1, 0), chip(1, 0)], True)
    event3(0)
    event3(1)
    shared(gathered.at[0, 0, c], 0)
    shared(gathered.at[0:2, 0:3, c], 2)
    add_scores([chip(0, 0), chip(0, 2), chip(-1, -1), chip(-1, 1), chip(1, -1), chip(1, 1)], False)
    event4(0)
    event4(1)
    shared(gathered.at[0, :, c], 3)
    add_scores([chip(2, 0), chip(1, 2), chip(-1, 2), chip(2, -1)], False)
    shared(gathered.at[0, 0, c], 4)
    finish([chip(2, 1), chip(2, 2)])

    locals_[4].wait()
    coef_high, coef_low = split2(cv[...])
    sk_high, sk_low = split2(skt[...])
    n_targets = cv.shape[0]
    first = mm(jnp.concatenate([coef_high, coef_low], axis=0), sk_high)
    predicted = first[:n_targets] + first[n_targets:] + mm(coef_high, sk_low)
    pred_send[...] = predicted.reshape(n_targets // 8, 8, structs)
    pred_recv[p] = pred_send[q]

    def exchange(src_slot, dst_slot, peer):
        return pltpu.make_async_remote_copy(
            src_ref=pred_send.at[src_slot],
            dst_ref=pred_recv.at[dst_slot],
            send_sem=late_sem.at[0],
            recv_sem=late_sem.at[1],
            device_id=peer,
            device_id_type=MESH,
        )

    n_plane = pred_recv.shape[0]

    far = sorted(range(1, n_plane), key=lambda i: -sum(min(v, NX - v) for v in (i // 2 // NX, i // 2 % NX)))
    for i in far:
        yi, xi = chip(i // 2 // NX, i // 2 % NX)
        peer = (yi * NX + xi) * 2 + (c if i % 2 == 0 else 1 - c)
        exchange(lax.div(peer, 4), p, (z, peer)).start()

    locals_[5].wait()
    settle(tz.at[pl.ds(0, NZ - 1)], late_sem.at[9], False)
    wanted = destv[pl.ds(z, 1), :]
    home = jnp.zeros((48, structs), F32)
    for owner in range(NZ):
        spots = lax.broadcasted_iota(jnp.int32, (structs, structs), 0) + owner * structs
        pick = jnp.where(spots == wanted, 1.0, 0.0).astype(BF16)
        home = home + mm(jnp.concatenate(split3(tz[owner]), axis=0), pick)
    home = (home[0:16] + home[16:32]) + home[32:48]
    turned = skt[...].T
    sk_high, sk_low = split2(turned)
    sht[...] = sk_high
    slt[...] = sk_low

    settle(pred_recv.at[pl.ds(0, n_plane - 1)], late_sem.at[1], False)
    summed = jnp.sum(pred_recv[...], axis=0)
    resid = home[8:16] * (summed - home[0:8])
    tiles[q] = resid

    def tile_copy(yi, xi):
        return pltpu.make_async_remote_copy(
            src_ref=tiles.at[q],
            dst_ref=tiles.at[q],
            send_sem=late_sem.at[2],
            recv_sem=late_sem.at[3],
            device_id=(z, (yi * NX + xi) * 2 + c),
            device_id_type=MESH,
        )

    for dy in (2, 1, 3, 0):
        yi = lax.rem(y + dy, NX)
        tile_copy(yi, NX - 1 - x).start()
        if dy:
            tile_copy(yi, x).start()
    mine = lax.rem(p, 4)
    out = resid[0:2]
    for j in range(1, 4):
        out = jnp.where(mine == j, resid[2 * j : 2 * j + 2], out)
    res_ref[...] = out
    settle(tiles.at[pl.ds(0, 7)], late_sem.at[3], False)

    res_high, res_low = split2(tiles[...].reshape(n_targets, structs))
    first = mm(jnp.concatenate([res_high, res_low], axis=0), sht[...])
    grads = first[:n_targets] + first[n_targets:] + mm(res_high, slt[...])
    grads = grads * (1.0 / (structs * NZ))
    share_rows = n_targets // NZ
    largest = jnp.max(jnp.max(jnp.abs(grads), axis=0, keepdims=True), axis=1, keepdims=True)
    largest = jnp.maximum(jnp.broadcast_to(largest, (1, 128)), 1e-30)
    step_send[...] = largest * (1.0 / CODES**2)
    to_one = jnp.broadcast_to(1.0 / largest, (n_targets, 128))
    to_one = jnp.concatenate([to_one] * (pivots // 128), axis=1)
    codes = jnp.floor(jnp.sqrt(jnp.abs(grads) * to_one) * CODES + 0.5)
    codes = jnp.where(grads < 0, -codes, codes).astype(jnp.int32)
    for owner in range(NZ):
        part = codes[owner * share_rows : (owner + 1) * share_rows]
        part = jnp.concatenate([part[:, k * 256 : (k + 1) * 256] for k in range(pivots // 256)], axis=0)
        grad_send[owner] = part.astype(jnp.int16)
    grad_recv[z] = grad_send[z]
    step_recv[z] = step_send[...]

    def send_grad(i, carry):
        peer = lax.rem(z + i, NZ)
        for src, dst, sem in (
            (grad_send.at[peer], grad_recv.at[z], 4),
            (step_send, step_recv.at[z], 6),
        ):
            pltpu.make_async_remote_copy(
                src_ref=src,
                dst_ref=dst,
                send_sem=late_sem.at[sem],
                recv_sem=late_sem.at[sem + 1],
                device_id=(peer, p),
                device_id_type=MESH,
            ).start()
        return carry

    for i in (8, 7, 9, 6, 10, 5, 11, 4, 12, 3, 13, 2, 14, 1, 15):
        send_grad(i, 0)

    settle(gathered.at[0, :, c], own_sem, True)
    settle(gathered.at[0:2, 0:3, c], line_sem, True)
    settle(gathered.at[0, 0, c], half_sem.at[0], True)
    settle(gathered.at[0, :, c], half_sem.at[1], True)
    settle(gathered.at[:, :, c], part_send_sem, True)
    settle(tz.at[pl.ds(0, NZ - 1)], late_sem.at[8], True)
    settle(pred_recv.at[pl.ds(0, n_plane - 1)], late_sem.at[0], True)
    settle(tiles.at[pl.ds(0, 7)], late_sem.at[2], True)
    settle(grad_recv.at[pl.ds(0, NZ - 1)], late_sem.at[5], False)
    settle(step_recv.at[pl.ds(0, NZ - 1)], late_sem.at[7], False)
    settle(step_recv.at[pl.ds(0, NZ - 1)], late_sem.at[6], True)
    total = jnp.zeros(grad_recv.shape[1:], F32)
    for src in range(NZ):
        scale = step_recv[src]
        scale = jnp.concatenate([scale, scale], axis=1)
        code = grad_recv[src].astype(jnp.int32).astype(F32)
        total = total + (code * jnp.abs(code)) * scale
    for k in range(pivots // 256):
        grad_ref[:, k * 256 : (k + 1) * 256] = total[k * share_rows : (k + 1) * share_rows]
    settle(grad_send.at[pl.ds(0, NZ - 1)], late_sem.at[4], True)


def on_device(descriptors, pivot_desc, coeffs, seg_ids, dest, targets, weights):
    atoms, rows = descriptors.shape
    pivots, width = pivot_desc.shape
    structs, n_targets = targets.shape
    any_spec = pl.BlockSpec(memory_space=pltpu.HBM)
    vmem_spec = pl.BlockSpec(memory_space=pltpu.VMEM)
    dma = pltpu.SemaphoreType.DMA
    res, grad = pl.pallas_call(
        kernel,
        out_shape=(
            pltpu.VMEM((n_targets // 32, structs), F32),
            pltpu.VMEM((n_targets // NZ, pivots), F32),
        ),
        in_specs=[any_spec] * 7,
        out_specs=(vmem_spec, vmem_spec),
        scratch_shapes=[
            pltpu.VMEM((NX, NX, 2, rows, atoms), BF16),
            pltpu.VMEM((pivots, width), BF16),
            pltpu.VMEM((n_targets, pivots), F32),
            pltpu.VMEM((1, atoms), jnp.int32),
            pltpu.VMEM((NZ, structs), jnp.int32),
            pltpu.VMEM((n_targets // 8, 8, structs), F32),
            pltpu.VMEM((1, structs), F32),
            pltpu.VMEM((pivots, 128), F32),
            pltpu.VMEM((atoms, structs), BF16),
            pltpu.VMEM((pivots, structs), F32),
            pltpu.VMEM((structs, pivots), BF16),
            pltpu.VMEM((structs, pivots), BF16),
            pltpu.VMEM((NZ, 16, structs), F32),
            pltpu.VMEM((n_targets // 8, 8, structs), F32),
            pltpu.VMEM((32, 8, structs), F32),
            pltpu.VMEM((n_targets // 8, 8, structs), F32),
            pltpu.VMEM((NZ, 16, 256), jnp.int16),
            pltpu.VMEM((NZ, 16, 256), jnp.int16),
            pltpu.VMEM((1, 128), F32),
            pltpu.VMEM((NZ, 1, 128), F32),
            pltpu.VMEM((8, atoms), F32),
            pltpu.VMEM((pivots, atoms), F32),
            dma((7,)),
            dma,
            dma,
            dma((2,)),
            dma,
            dma((20, NB)),
            dma((5,)),
            pltpu.SemaphoreType.REGULAR((3,)),
            dma((10,)),
        ],
        compiler_params=pltpu.CompilerParams(
            collective_id=0, has_side_effects=True, vmem_limit_bytes=60 * 1024 * 1024
        ),
        name="fit_gradient",
    )(
        descriptors.T,
        pivot_desc,
        coeffs.T,
        seg_ids,
        dest.reshape(NZ, structs),
        targets.T.reshape(n_targets // 8, 8, structs),
        weights.reshape(1, structs),
    )
    return res.T, grad


def solution(mesh):
    placed = (
        P("atoms", "pivots"),
        P("pivots", None),
        P("pivots", None),
        P("atoms", None),
        P(),
        P("atoms", None),
        P("atoms"),
    )
    return jax.shard_map(
        on_device,
        mesh=mesh,
        in_specs=placed,
        out_specs=(P("atoms", "pivots"), P("atoms", "pivots")),
        check_vma=False,
    )
```

```python
import functools

import jax
import jax.numpy as jnp
from jax import lax
from jax.experimental import pallas as pl
from jax.experimental.pallas import tpu as pltpu
from jax.sharding import PartitionSpec as P

EPS = 1e-6
MESH = pl.DeviceIdType.MESH
F32 = jnp.float32
BF16 = jnp.bfloat16
CODES = 32766.0
NB = 2
NZ = 16
NX = 4


def split2(value):
    high = value.astype(BF16)
    low = (value - high.astype(F32)).astype(BF16)
    return high, low


def split3(value):
    high = value.astype(BF16)
    rest = value - high.astype(F32)
    mid = rest.astype(BF16)
    low = (rest - mid.astype(F32)).astype(BF16)
    return high, mid, low


def mm(left, right):
    return jnp.dot(left, right, preferred_element_type=F32)


def kernel(
    d_ref,
    p_ref,
    c_ref,
    seg_ref,
    dest_ref,
    tgt_ref,
    w_ref,
    res_ref,
    grad_ref,
    gathered,
    pv,
    cv,
    segv,
    destv,
    tgtv,
    wv,
    p2,
    members,
    skt,
    sht,
    slt,
    tz,
    pred_send,
    pred_recv,
    tiles,
    grad_send,
    grad_recv,
    step_send,
    step_recv,
    squares,
    scores,
    local_sem,
    own_sem,
    line_sem,
    half_sem,
    part_send_sem,
    recv_sem,
    part_recv_sem,
    known_sem,
    late_sem,
):
    z = lax.axis_index("atoms")
    p = lax.axis_index("pivots")
    c = lax.rem(p, 2)
    x = lax.rem(lax.div(p, 2), NX)
    y = lax.div(p, 2 * NX)
    q = lax.div(p, 4)
    rows = d_ref.shape[0]
    half = rows // 2
    atoms = d_ref.shape[1]
    width = atoms // NB
    pivots = p_ref.shape[0]
    tile = pivots // 4
    structs = tz.shape[2]

    def wrap(value):
        return lax.rem(value + NX, NX)

    def place(f, s):
        return wrap(y + s * (1 - c) + f * c), wrap(x + f * (1 - c) + s * c)

    def device(f, s):
        yi, xi = place(f, s)
        return (z, (yi * NX + xi) * 2 + c)

    partner = (z, p + 1 - 2 * c)
    up = (lax.rem(z + 1, NZ), p)
    down = (lax.rem(z + NZ - 1, NZ), p)
    f_up, f_down = device(1, 0), device(-1, 0)
    s_up, s_down = device(0, 1), device(0, -1)

    locals_ = [
        pltpu.make_async_copy(tgt_ref, tgtv, local_sem.at[0]),
        pltpu.make_async_copy(w_ref, wv, local_sem.at[1]),
        pltpu.make_async_copy(seg_ref, segv, local_sem.at[2]),
        pltpu.make_async_copy(p_ref, pv, local_sem.at[3]),
        pltpu.make_async_copy(c_ref, cv, local_sem.at[4]),
        pltpu.make_async_copy(dest_ref, destv, local_sem.at[5]),
        pltpu.make_async_copy(d_ref, gathered.at[y, x, c], local_sem.at[6]),
    ]
    barrier = pltpu.get_barrier_semaphore()
    for peer in (f_up, f_down, s_up, s_down, partner, up, down):
        pl.semaphore_signal(barrier, inc=1, device_id=peer, device_id_type=MESH)
    locals_[6].start()
    for k in (0, 1, 2):
        locals_[k].start()
    pl.semaphore_wait(barrier, 7)

    def span(b):
        return pl.ds(pl.multiple_of(b * width, width), width)

    def own(b):
        for kind, peer in ((0, f_up), (1, f_down), (2, s_up), (3, s_down)):
            pltpu.make_async_remote_copy(
                src_ref=gathered.at[y, x, c, :, span(b)],
                dst_ref=gathered.at[y, x, c, :, span(b)],
                send_sem=own_sem,
                recv_sem=recv_sem.at[kind, b],
                device_id=peer,
                device_id_type=MESH,
            ).start()
        pltpu.make_async_remote_copy(
            src_ref=gathered.at[y, x, c, :, span(b)],
            dst_ref=gathered.at[y, x, c, :, span(b)],
            send_sem=part_send_sem,
            recv_sem=part_recv_sem.at[0],
            device_id=partner,
            device_id_type=MESH,
        ).start()

    locals_[6].wait()
    for b in range(NB):
        own(b)
    for k in (3, 4, 5):
        locals_[k].start()

    def piece(spot, part, b):
        yi, xi = spot
        return gathered.at[yi, xi, c, part, span(b)]

    whole, low, high = pl.ds(0, rows), pl.ds(0, half), pl.ds(half, half)

    def forward(kind, b, spot, part, sem, peer):
        ref = piece(spot, part, b)
        pltpu.make_async_remote_copy(
            src_ref=ref,
            dst_ref=ref,
            send_sem=sem,
            recv_sem=recv_sem.at[kind, b],
            device_id=peer,
            device_id_type=MESH,
        ).start()

    def share(b, spot, group):
        ref = piece(spot, whole, b)
        pltpu.make_async_remote_copy(
            src_ref=ref,
            dst_ref=ref,
            send_sem=part_send_sem,
            recv_sem=part_recv_sem.at[group],
            device_id=partner,
            device_id_type=MESH,
        ).start()

    def arrive(kind, b, spot, part):
        ref = piece(spot, part, b)
        pltpu.make_async_remote_copy(
            src_ref=ref,
            dst_ref=ref,
            send_sem=own_sem,
            recv_sem=recv_sem.at[kind, b],
            device_id=partner,
            device_id_type=MESH,
        ).wait_recv()

    to_low, to_high = half_sem.at[0], half_sem.at[1]

    def event1(b):
        spot = place(-1, 0)
        arrive(0, b, spot, whole)
        forward(4, b, spot, low, to_low, f_up)
        forward(6, b, spot, whole, line_sem, s_up)
        forward(7, b, spot, whole, line_sem, s_down)
        share(b, spot, 1)
        spot = place(1, 0)
        arrive(1, b, spot, whole)
        forward(5, b, spot, high, to_low, f_down)
        forward(8, b, spot, whole, line_sem, s_up)
        forward(9, b, spot, whole, line_sem, s_down)
        share(b, spot, 1)
        spot = place(0, -1)
        arrive(2, b, spot, whole)
        forward(12, b, spot, low, to_high, s_up)
        share(b, spot, 1)
        spot = place(0, 1)
        arrive(3, b, spot, whole)
        forward(13, b, spot, high, to_high, s_down)
        share(b, spot, 1)

    def event2(b):
        spot = place(2, 0)
        arrive(4, b, spot, low)
        arrive(5, b, spot, high)
        forward(10, b, spot, whole, line_sem, s_up)
        forward(11, b, spot, whole, line_sem, s_down)
        share(b, spot, 2)
        for f, first in ((-1, 6), (1, 8)):
            spot = place(f, -1)
            arrive(first, b, spot, whole)
            forward(first + 8, b, spot, low, to_high, s_up)
            share(b, spot, 2)
            spot = place(f, 1)
            arrive(first + 1, b, spot, whole)
            forward(first + 9, b, spot, high, to_high, s_down)
            share(b, spot, 2)
        spot = place(0, 2)
        arrive(12, b, spot, low)
        arrive(13, b, spot, high)
        share(b, spot, 2)

    def event3(b):
        spot = place(2, -1)
        arrive(10, b, spot, whole)
        forward(18, b, spot, low, to_high, s_up)
        share(b, spot, 3)
        spot = place(2, 1)
        arrive(11, b, spot, whole)
        forward(19, b, spot, high, to_high, s_down)
        share(b, spot, 3)
        for f, first in ((-1, 14), (1, 16)):
            spot = place(f, 2)
            arrive(first, b, spot, low)
            arrive(first + 1, b, spot, high)
            share(b, spot, 3)

    def event4(b):
        spot = place(2, 2)
        arrive(18, b, spot, low)
        arrive(19, b, spot, high)
        share(b, spot, 4)

    def shared(ref, group):
        pltpu.make_async_remote_copy(
            src_ref=ref,
            dst_ref=ref,
            send_sem=own_sem,
            recv_sem=part_recv_sem.at[group],
            device_id=partner,
            device_id_type=MESH,
        ).wait_recv()

    def greet(distance, step):
        for peer in (lax.rem(z + distance, NZ), lax.rem(z + NZ - distance, NZ)):
            pl.semaphore_signal(known_sem.at[step], inc=1, device_id=(peer, p), device_id_type=MESH)

    greet(1, 0)

    locals_[0].wait()
    locals_[1].wait()
    tz[z, 0:8, :] = tgtv[q]
    tz[z, 8:16, :] = jnp.broadcast_to(wv[...], (8, structs))

    locals_[2].wait()
    ids = lax.broadcasted_iota(jnp.int32, (structs, atoms), 0)
    chosen = jnp.where(ids == segv[...], 1.0, 0.0).astype(F32)
    members[...] = chosen.T.astype(BF16)

    def pivot_scales(k):
        at = pl.ds(pl.multiple_of(k * tile, tile), tile)
        total = jnp.zeros((tile, 128), F32)
        for j in range(pv.shape[1] // 128):
            part = pv[at, j * 128 : (j + 1) * 128].astype(F32)
            total = total + part * part
        scale = lax.rsqrt(jnp.sum(total, axis=1, keepdims=True) + EPS)
        squared = (desc_width * scale) * scale
        p2[at, :] = jnp.broadcast_to(squared, (tile, 128))

    desc_width = float(pv.shape[1])

    def chip(dy, dx):
        return wrap(y + dy), wrap(x + dx)

    def operand(chips):
        parts = [gathered[yi, xi].reshape(2 * rows, atoms) for yi, xi in chips]
        return jnp.concatenate(parts, axis=0)

    def columns(at, chips):
        parts = []
        for yi, xi in chips:
            first = pl.multiple_of((yi * NX + xi) * 2 * rows, 128)
            parts.append(pv[at, pl.ds(first, 2 * rows)])
        return jnp.concatenate(parts, axis=1)

    def add_squares(chips, start):
        total = jnp.zeros((8, atoms), F32) if start else squares[...]
        for yi, xi in chips:
            part = gathered[yi, xi].astype(F32)
            part = (part * part).reshape(2 * rows // 8, 8, atoms)
            total = total + jnp.sum(part, axis=0)
        squares[...] = total

    def add_scores(chips, start):
        right = operand(chips)
        for j in range(pivots // tile):
            at = pl.ds(j * tile, tile)
            part = mm(columns(at, chips), right)
            scores[at, :] = part if start else scores[at, :] + part
        add_squares(chips, start)

    def finish(chips):
        add_squares(chips, False)
        row = lax.rsqrt(jnp.sum(squares[...], axis=0, keepdims=True) + EPS)
        right = operand(chips)
        for j in range(pivots // tile):
            at = pl.ds(j * tile, tile)
            scaled = (scores[at, :] + mm(columns(at, chips), right)) * row
            scaled = scaled * scaled
            factor = jnp.concatenate([p2[at, :]] * (atoms // 128), axis=1)
            entries = (scaled * factor).astype(BF16)
            skt[at, :] = mm(entries, members[...])

    def settle(ref, sem, sending):
        copy = pltpu.make_async_remote_copy(
            src_ref=ref,
            dst_ref=ref,
            send_sem=sem,
            recv_sem=sem,
            device_id=partner,
            device_id_type=MESH,
        )
        if sending:
            copy.wait_send()
        else:
            copy.wait_recv()

    def send_owner(i):
        pltpu.make_async_remote_copy(
            src_ref=tz.at[z],
            dst_ref=tz.at[z],
            send_sem=late_sem.at[8],
            recv_sem=late_sem.at[9],
            device_id=(lax.rem(z + i, NZ), p),
            device_id_type=MESH,
        ).start()

    locals_[3].wait()
    for k in range(pivots // tile):
        pivot_scales(k)
    event1(0)
    pl.semaphore_wait(known_sem.at[0], 2)
    greet(2, 1)
    event1(1)
    pl.semaphore_wait(known_sem.at[1], 2)
    greet(4, 2)
    event2(0)
    event2(1)
    pl.semaphore_wait(known_sem.at[2], 2)
    for i in (8, 7, 9, 6, 10, 5, 11, 4, 12, 3, 13, 2, 14, 1, 15):
        send_owner(i)
    shared(gathered.at[0, :, c], 1)
    add_scores([chip(0, -1), chip(0, 1), chip(-1, 0), chip(1, 0)], True)
    event3(0)
    event3(1)
    shared(gathered.at[0, 0, c], 0)
    shared(gathered.at[0:2, 0:3, c], 2)
    add_scores([chip(0, 0), chip(0, 2), chip(-1, -1), chip(-1, 1), chip(1, -1), chip(1, 1)], False)
    event4(0)
    event4(1)
    shared(gathered.at[0, :, c], 3)
    add_scores([chip(2, 0), chip(1, 2), chip(-1, 2), chip(2, -1)], False)
    shared(gathered.at[0, 0, c], 4)
    finish([chip(2, 1), chip(2, 2)])

    locals_[4].wait()
    coef_high, coef_low = split2(cv[...])
    sk_high, sk_low = split2(skt[...])
    n_targets = cv.shape[0]
    first = mm(jnp.concatenate([coef_high, coef_low], axis=0), sk_high)
    predicted = first[:n_targets] + first[n_targets:] + mm(coef_high, sk_low)
    pred_send[...] = predicted.reshape(n_targets // 8, 8, structs)
    pred_recv[p] = pred_send[q]

    def exchange(src_slot, dst_slot, peer):
        return pltpu.make_async_remote_copy(
            src_ref=pred_send.at[src_slot],
            dst_ref=pred_recv.at[dst_slot],
            send_sem=late_sem.at[0],
            recv_sem=late_sem.at[1],
            device_id=peer,
            device_id_type=MESH,
        )

    n_plane = pred_recv.shape[0]

    far = sorted(range(1, n_plane), key=lambda i: -sum(min(v, NX - v) for v in (i // 2 // NX, i // 2 % NX)))
    for i in far:
        yi, xi = chip(i // 2 // NX, i // 2 % NX)
        peer = (yi * NX + xi) * 2 + (c if i % 2 == 0 else 1 - c)
        exchange(lax.div(peer, 4), p, (z, peer)).start()

    locals_[5].wait()
    settle(tz.at[pl.ds(0, NZ - 1)], late_sem.at[9], False)
    wanted = destv[pl.ds(z, 1), :]
    home = jnp.zeros((48, structs), F32)
    for owner in range(NZ):
        spots = lax.broadcasted_iota(jnp.int32, (structs, structs), 0) + owner * structs
        pick = jnp.where(spots == wanted, 1.0, 0.0).astype(BF16)
        home = home + mm(jnp.concatenate(split3(tz[owner]), axis=0), pick)
    home = (home[0:16] + home[16:32]) + home[32:48]
    turned = skt[...].T
    sk_high, sk_low = split2(turned)
    sht[...] = sk_high
    slt[...] = sk_low

    settle(pred_recv.at[pl.ds(0, n_plane - 1)], late_sem.at[1], False)
    summed = jnp.sum(pred_recv[...], axis=0)
    resid = home[8:16] * (summed - home[0:8])
    tiles[q] = resid

    def tile_copy(yi, xi):
        return pltpu.make_async_remote_copy(
            src_ref=tiles.at[q],
            dst_ref=tiles.at[q],
            send_sem=late_sem.at[2],
            recv_sem=late_sem.at[3],
            device_id=(z, (yi * NX + xi) * 2 + c),
            device_id_type=MESH,
        )

    for dy in (2, 1, 3, 0):
        yi = lax.rem(y + dy, NX)
        tile_copy(yi, NX - 1 - x).start()
        if dy:
            tile_copy(yi, x).start()
    mine = lax.rem(p, 4)
    out = resid[0:2]
    for j in range(1, 4):
        out = jnp.where(mine == j, resid[2 * j : 2 * j + 2], out)
    res_ref[...] = out
    settle(tiles.at[pl.ds(0, 7)], late_sem.at[3], False)

    res_high, res_low = split2(tiles[...].reshape(n_targets, structs))
    first = mm(jnp.concatenate([res_high, res_low], axis=0), sht[...])
    grads = first[:n_targets] + first[n_targets:] + mm(res_high, slt[...])
    grads = grads * (1.0 / (structs * NZ))
    share_rows = n_targets // NZ
    largest = jnp.max(jnp.max(jnp.abs(grads), axis=0, keepdims=True), axis=1, keepdims=True)
    largest = jnp.maximum(jnp.broadcast_to(largest, (1, 128)), 1e-30)
    step_send[...] = largest * (1.0 / CODES**2)
    to_one = jnp.broadcast_to(1.0 / largest, (n_targets, 128))
    to_one = jnp.concatenate([to_one] * (pivots // 128), axis=1)
    codes = jnp.floor(jnp.sqrt(jnp.abs(grads) * to_one) * CODES + 0.5)
    codes = jnp.where(grads < 0, -codes, codes).astype(jnp.int32)
    for owner in range(NZ):
        part = codes[owner * share_rows : (owner + 1) * share_rows]
        part = jnp.concatenate([part[:, k * 256 : (k + 1) * 256] for k in range(pivots // 256)], axis=0)
        grad_send[owner] = part.astype(jnp.int16)
    grad_recv[z] = grad_send[z]
    step_recv[z] = step_send[...]

    def send_grad(i, carry):
        peer = lax.rem(z + i, NZ)
        for src, dst, sem in (
            (grad_send.at[peer], grad_recv.at[z], 4),
            (step_send, step_recv.at[z], 6),
        ):
            pltpu.make_async_remote_copy(
                src_ref=src,
                dst_ref=dst,
                send_sem=late_sem.at[sem],
                recv_sem=late_sem.at[sem + 1],
                device_id=(peer, p),
                device_id_type=MESH,
            ).start()
        return carry

    for i in (8, 7, 9, 6, 10, 5, 11, 4, 12, 3, 13, 2, 14, 1, 15):
        send_grad(i, 0)

    settle(gathered.at[0, :, c], own_sem, True)
    settle(gathered.at[0:2, 0:3, c], line_sem, True)
    settle(gathered.at[0, 0, c], half_sem.at[0], True)
    settle(gathered.at[0, :, c], half_sem.at[1], True)
    settle(gathered.at[:, :, c], part_send_sem, True)
    settle(tz.at[pl.ds(0, NZ - 1)], late_sem.at[8], True)
    settle(pred_recv.at[pl.ds(0, n_plane - 1)], late_sem.at[0], True)
    settle(tiles.at[pl.ds(0, 7)], late_sem.at[2], True)
    settle(grad_recv.at[pl.ds(0, NZ - 1)], late_sem.at[5], False)
    settle(step_recv.at[pl.ds(0, NZ - 1)], late_sem.at[7], False)
    settle(step_recv.at[pl.ds(0, NZ - 1)], late_sem.at[6], True)
    total = jnp.zeros(grad_recv.shape[1:], F32)
    for src in range(NZ):
        scale = step_recv[src]
        scale = jnp.concatenate([scale, scale], axis=1)
        code = grad_recv[src].astype(jnp.int32).astype(F32)
        total = total + (code * jnp.abs(code)) * scale
    for k in range(pivots // 256):
        grad_ref[:, k * 256 : (k + 1) * 256] = total[k * share_rows : (k + 1) * share_rows]
    settle(grad_send.at[pl.ds(0, NZ - 1)], late_sem.at[4], True)


def store(res_ref, grad_ref, res_out, grad_out, sem):
    copies = [
        pltpu.make_async_copy(res_ref, res_out, sem.at[0]),
        pltpu.make_async_copy(grad_ref, grad_out, sem.at[1]),
    ]
    for copy in copies:
        copy.start()
    for copy in copies:
        copy.wait()


def on_device(descriptors, pivot_desc, coeffs, seg_ids, dest, targets, weights):
    atoms, rows = descriptors.shape
    pivots, width = pivot_desc.shape
    structs, n_targets = targets.shape
    any_spec = pl.BlockSpec(memory_space=pltpu.HBM)
    vmem_spec = pl.BlockSpec(memory_space=pltpu.VMEM)
    dma = pltpu.SemaphoreType.DMA
    res, grad = pl.pallas_call(
        kernel,
        out_shape=(
            pltpu.VMEM((n_targets // 32, structs), F32),
            pltpu.VMEM((n_targets // NZ, pivots), F32),
        ),
        in_specs=[any_spec] * 7,
        out_specs=(vmem_spec, vmem_spec),
        scratch_shapes=[
            pltpu.VMEM((NX, NX, 2, rows, atoms), BF16),
            pltpu.VMEM((pivots, width), BF16),
            pltpu.VMEM((n_targets, pivots), F32),
            pltpu.VMEM((1, atoms), jnp.int32),
            pltpu.VMEM((NZ, structs), jnp.int32),
            pltpu.VMEM((n_targets // 8, 8, structs), F32),
            pltpu.VMEM((1, structs), F32),
            pltpu.VMEM((pivots, 128), F32),
            pltpu.VMEM((atoms, structs), BF16),
            pltpu.VMEM((pivots, structs), F32),
            pltpu.VMEM((structs, pivots), BF16),
            pltpu.VMEM((structs, pivots), BF16),
            pltpu.VMEM((NZ, 16, structs), F32),
            pltpu.VMEM((n_targets // 8, 8, structs), F32),
            pltpu.VMEM((32, 8, structs), F32),
            pltpu.VMEM((n_targets // 8, 8, structs), F32),
            pltpu.VMEM((NZ, 16, 256), jnp.int16),
            pltpu.VMEM((NZ, 16, 256), jnp.int16),
            pltpu.VMEM((1, 128), F32),
            pltpu.VMEM((NZ, 1, 128), F32),
            pltpu.VMEM((8, atoms), F32),
            pltpu.VMEM((pivots, atoms), F32),
            dma((7,)),
            dma,
            dma,
            dma((2,)),
            dma,
            dma((20, NB)),
            dma((5,)),
            pltpu.SemaphoreType.REGULAR((3,)),
            dma((10,)),
        ],
        compiler_params=pltpu.CompilerParams(
            collective_id=0, has_side_effects=True, vmem_limit_bytes=60 * 1024 * 1024
        ),
        name="fit_gradient",
    )(
        descriptors.T,
        pivot_desc,
        coeffs.T,
        seg_ids,
        dest.reshape(NZ, structs),
        targets.T.reshape(n_targets // 8, 8, structs),
        weights.reshape(1, structs),
    )
    res, grad = pl.pallas_call(
        store,
        out_shape=(
            jax.ShapeDtypeStruct(res.shape, F32),
            jax.ShapeDtypeStruct(grad.shape, F32),
        ),
        in_specs=[vmem_spec, vmem_spec],
        out_specs=(any_spec, any_spec),
        scratch_shapes=[dma((2,))],
        name="store_results",
    )(
        pltpu.with_memory_space_constraint(res, pltpu.VMEM),
        pltpu.with_memory_space_constraint(grad, pltpu.VMEM),
    )
    return res.T, grad


def solution(mesh):
    placed = (
        P("atoms", "pivots"),
        P("pivots", None),
        P("pivots", None),
        P("atoms", None),
        P(),
        P("atoms", None),
        P("atoms"),
    )
    return jax.shard_map(
        on_device,
        mesh=mesh,
        in_specs=placed,
        out_specs=(P("atoms", "pivots"), P("atoms", "pivots")),
        check_vma=False,
    )
```

```python
import functools

import jax
import jax.numpy as jnp
from jax import lax
from jax.experimental import pallas as pl
from jax.experimental.pallas import tpu as pltpu
from jax.sharding import PartitionSpec as P

EPS = 1e-6
MESH = pl.DeviceIdType.MESH
F32 = jnp.float32
BF16 = jnp.bfloat16
CODES = 32766.0
NB = 2
NZ = 16
NX = 4


def split2(value):
    high = value.astype(BF16)
    low = (value - high.astype(F32)).astype(BF16)
    return high, low


def split3(value):
    high = value.astype(BF16)
    rest = value - high.astype(F32)
    mid = rest.astype(BF16)
    low = (rest - mid.astype(F32)).astype(BF16)
    return high, mid, low


def mm(left, right):
    return jnp.dot(left, right, preferred_element_type=F32)


def kernel(
    d_ref,
    p_ref,
    c_ref,
    seg_ref,
    dest_ref,
    tgt_ref,
    w_ref,
    res_ref,
    grad_ref,
    gathered,
    pv,
    cv,
    segv,
    destv,
    tgtv,
    wv,
    p2,
    members,
    skt,
    sht,
    slt,
    tz,
    pred_send,
    pred_recv,
    tiles,
    grad_send,
    grad_recv,
    step_send,
    step_recv,
    squares,
    scores,
    local_sem,
    own_sem,
    line_sem,
    half_sem,
    part_send_sem,
    recv_sem,
    part_recv_sem,
    known_sem,
    late_sem,
):
    z = lax.axis_index("atoms")
    p = lax.axis_index("pivots")
    c = lax.rem(p, 2)
    x = lax.rem(lax.div(p, 2), NX)
    y = lax.div(p, 2 * NX)
    q = lax.div(p, 4)
    rows = d_ref.shape[0]
    half = rows // 2
    atoms = d_ref.shape[1]
    width = atoms // NB
    pivots = p_ref.shape[0]
    tile = pivots // 4
    structs = tz.shape[2]

    def wrap(value):
        return lax.rem(value + NX, NX)

    def place(f, s):
        return wrap(y + s * (1 - c) + f * c), wrap(x + f * (1 - c) + s * c)

    def device(f, s):
        yi, xi = place(f, s)
        return (z, (yi * NX + xi) * 2 + c)

    partner = (z, p + 1 - 2 * c)
    up = (lax.rem(z + 1, NZ), p)
    down = (lax.rem(z + NZ - 1, NZ), p)
    f_up, f_down = device(1, 0), device(-1, 0)
    s_up, s_down = device(0, 1), device(0, -1)

    locals_ = [
        pltpu.make_async_copy(tgt_ref, tgtv, local_sem.at[0]),
        pltpu.make_async_copy(w_ref, wv, local_sem.at[1]),
        pltpu.make_async_copy(seg_ref, segv, local_sem.at[2]),
        pltpu.make_async_copy(p_ref, pv, local_sem.at[3]),
        pltpu.make_async_copy(c_ref, cv, local_sem.at[4]),
        pltpu.make_async_copy(dest_ref, destv, local_sem.at[5]),
        pltpu.make_async_copy(d_ref, gathered.at[y, x, c], local_sem.at[6]),
    ]
    barrier = pltpu.get_barrier_semaphore()
    for peer in (f_up, f_down, s_up, s_down, partner, up, down):
        pl.semaphore_signal(barrier, inc=1, device_id=peer, device_id_type=MESH)
    locals_[6].start()
    for k in (0, 1, 2):
        locals_[k].start()
    pl.semaphore_wait(barrier, 7)

    def span(b):
        return pl.ds(pl.multiple_of(b * width, width), width)

    def own(b):
        for kind, peer in ((0, f_up), (1, f_down), (2, s_up), (3, s_down)):
            pltpu.make_async_remote_copy(
                src_ref=gathered.at[y, x, c, :, span(b)],
                dst_ref=gathered.at[y, x, c, :, span(b)],
                send_sem=own_sem,
                recv_sem=recv_sem.at[kind, b],
                device_id=peer,
                device_id_type=MESH,
            ).start()
        pltpu.make_async_remote_copy(
            src_ref=gathered.at[y, x, c, :, span(b)],
            dst_ref=gathered.at[y, x, c, :, span(b)],
            send_sem=part_send_sem,
            recv_sem=part_recv_sem.at[0],
            device_id=partner,
            device_id_type=MESH,
        ).start()

    locals_[6].wait()
    for b in range(NB):
        own(b)
    for k in (3, 4, 5):
        locals_[k].start()

    def piece(spot, part, b):
        yi, xi = spot
        return gathered.at[yi, xi, c, part, span(b)]

    whole, low, high = pl.ds(0, rows), pl.ds(0, half), pl.ds(half, half)

    def forward(kind, b, spot, part, sem, peer):
        ref = piece(spot, part, b)
        pltpu.make_async_remote_copy(
            src_ref=ref,
            dst_ref=ref,
            send_sem=sem,
            recv_sem=recv_sem.at[kind, b],
            device_id=peer,
            device_id_type=MESH,
        ).start()

    def share(b, spot, group):
        ref = piece(spot, whole, b)
        pltpu.make_async_remote_copy(
            src_ref=ref,
            dst_ref=ref,
            send_sem=part_send_sem,
            recv_sem=part_recv_sem.at[group],
            device_id=partner,
            device_id_type=MESH,
        ).start()

    def arrive(kind, b, spot, part):
        ref = piece(spot, part, b)
        pltpu.make_async_remote_copy(
            src_ref=ref,
            dst_ref=ref,
            send_sem=own_sem,
            recv_sem=recv_sem.at[kind, b],
            device_id=partner,
            device_id_type=MESH,
        ).wait_recv()

    to_low, to_high = half_sem.at[0], half_sem.at[1]

    def event1(b):
        before, after = place(-1, 0), place(1, 0)
        arrive(0, b, before, whole)
        forward(4, b, before, low, to_low, f_up)
        arrive(1, b, after, whole)
        forward(5, b, after, high, to_low, f_down)
        forward(6, b, before, whole, line_sem, s_up)
        forward(7, b, before, whole, line_sem, s_down)
        forward(8, b, after, whole, line_sem, s_up)
        forward(9, b, after, whole, line_sem, s_down)
        share(b, before, 1)
        share(b, after, 1)
        spot = place(0, -1)
        arrive(2, b, spot, whole)
        forward(12, b, spot, low, to_high, s_up)
        share(b, spot, 1)
        spot = place(0, 1)
        arrive(3, b, spot, whole)
        forward(13, b, spot, high, to_high, s_down)
        share(b, spot, 1)

    def event2(b):
        spot = place(2, 0)
        arrive(4, b, spot, low)
        arrive(5, b, spot, high)
        forward(10, b, spot, whole, line_sem, s_up)
        forward(11, b, spot, whole, line_sem, s_down)
        share(b, spot, 2)
        for f, first in ((-1, 6), (1, 8)):
            spot = place(f, -1)
            arrive(first, b, spot, whole)
            forward(first + 8, b, spot, low, to_high, s_up)
            share(b, spot, 2)
            spot = place(f, 1)
            arrive(first + 1, b, spot, whole)
            forward(first + 9, b, spot, high, to_high, s_down)
            share(b, spot, 2)
        spot = place(0, 2)
        arrive(12, b, spot, low)
        arrive(13, b, spot, high)
        share(b, spot, 2)

    def event3(b):
        spot = place(2, -1)
        arrive(10, b, spot, whole)
        forward(18, b, spot, low, to_high, s_up)
        share(b, spot, 3)
        spot = place(2, 1)
        arrive(11, b, spot, whole)
        forward(19, b, spot, high, to_high, s_down)
        share(b, spot, 3)
        for f, first in ((-1, 14), (1, 16)):
            spot = place(f, 2)
            arrive(first, b, spot, low)
            arrive(first + 1, b, spot, high)
            share(b, spot, 3)

    def event4(b):
        spot = place(2, 2)
        arrive(18, b, spot, low)
        arrive(19, b, spot, high)
        share(b, spot, 4)

    def shared(ref, group):
        pltpu.make_async_remote_copy(
            src_ref=ref,
            dst_ref=ref,
            send_sem=own_sem,
            recv_sem=part_recv_sem.at[group],
            device_id=partner,
            device_id_type=MESH,
        ).wait_recv()

    def greet(distance, step):
        for peer in (lax.rem(z + distance, NZ), lax.rem(z + NZ - distance, NZ)):
            pl.semaphore_signal(known_sem.at[step], inc=1, device_id=(peer, p), device_id_type=MESH)

    greet(1, 0)

    locals_[0].wait()
    locals_[1].wait()
    tz[z, 0:8, :] = tgtv[q]
    tz[z, 8:16, :] = jnp.broadcast_to(wv[...], (8, structs))

    locals_[2].wait()
    ids = lax.broadcasted_iota(jnp.int32, (structs, atoms), 0)
    chosen = jnp.where(ids == segv[...], 1.0, 0.0).astype(F32)
    members[...] = chosen.T.astype(BF16)

    def pivot_scales(k):
        at = pl.ds(pl.multiple_of(k * tile, tile), tile)
        total = jnp.zeros((tile, 128), F32)
        for j in range(pv.shape[1] // 128):
            part = pv[at, j * 128 : (j + 1) * 128].astype(F32)
            total = total + part * part
        scale = lax.rsqrt(jnp.sum(total, axis=1, keepdims=True) + EPS)
        squared = (desc_width * scale) * scale
        p2[at, :] = jnp.broadcast_to(squared, (tile, 128))

    desc_width = float(pv.shape[1])

    def chip(dy, dx):
        return wrap(y + dy), wrap(x + dx)

    def operand(chips):
        parts = [gathered[yi, xi].reshape(2 * rows, atoms) for yi, xi in chips]
        return jnp.concatenate(parts, axis=0)

    def columns(at, chips):
        parts = []
        for yi, xi in chips:
            first = pl.multiple_of((yi * NX + xi) * 2 * rows, 128)
            parts.append(pv[at, pl.ds(first, 2 * rows)])
        return jnp.concatenate(parts, axis=1)

    def add_squares(chips, start):
        total = jnp.zeros((8, atoms), F32) if start else squares[...]
        for yi, xi in chips:
            part = gathered[yi, xi].astype(F32)
            part = (part * part).reshape(2 * rows // 8, 8, atoms)
            total = total + jnp.sum(part, axis=0)
        squares[...] = total

    def add_scores(chips, start):
        right = operand(chips)
        for j in range(pivots // tile):
            at = pl.ds(j * tile, tile)
            part = mm(columns(at, chips), right)
            scores[at, :] = part if start else scores[at, :] + part
        add_squares(chips, start)

    def finish(chips):
        add_squares(chips, False)
        row = lax.rsqrt(jnp.sum(squares[...], axis=0, keepdims=True) + EPS)
        right = operand(chips)
        for j in range(pivots // tile):
            at = pl.ds(j * tile, tile)
            scaled = (scores[at, :] + mm(columns(at, chips), right)) * row
            scaled = scaled * scaled
            factor = jnp.concatenate([p2[at, :]] * (atoms // 128), axis=1)
            entries = (scaled * factor).astype(BF16)
            skt[at, :] = mm(entries, members[...])

    def settle(ref, sem, sending):
        copy = pltpu.make_async_remote_copy(
            src_ref=ref,
            dst_ref=ref,
            send_sem=sem,
            recv_sem=sem,
            device_id=partner,
            device_id_type=MESH,
        )
        if sending:
            copy.wait_send()
        else:
            copy.wait_recv()

    def send_owner(i):
        pltpu.make_async_remote_copy(
            src_ref=tz.at[z],
            dst_ref=tz.at[z],
            send_sem=late_sem.at[8],
            recv_sem=late_sem.at[9],
            device_id=(lax.rem(z + i, NZ), p),
            device_id_type=MESH,
        ).start()

    locals_[3].wait()
    for k in range(pivots // tile):
        pivot_scales(k)
    event1(0)
    pl.semaphore_wait(known_sem.at[0], 2)
    greet(2, 1)
    event1(1)
    pl.semaphore_wait(known_sem.at[1], 2)
    greet(4, 2)
    event2(0)
    event2(1)
    pl.semaphore_wait(known_sem.at[2], 2)
    for i in (8, 7, 9, 6, 10, 5, 11, 4, 12, 3, 13, 2, 14, 1, 15):
        send_owner(i)
    shared(gathered.at[0, :, c], 1)
    add_scores([chip(0, -1), chip(0, 1), chip(-1, 0), chip(1, 0)], True)
    event3(0)
    event3(1)
    shared(gathered.at[0, 0, c], 0)
    shared(gathered.at[0:2, 0:3, c], 2)
    add_scores([chip(0, 0), chip(0, 2), chip(-1, -1), chip(-1, 1), chip(1, -1), chip(1, 1)], False)
    event4(0)
    event4(1)
    shared(gathered.at[0, :, c], 3)
    add_scores([chip(2, 0), chip(1, 2), chip(-1, 2), chip(2, -1)], False)
    shared(gathered.at[0, 0, c], 4)
    finish([chip(2, 1), chip(2, 2)])

    locals_[4].wait()
    coef_high, coef_low = split2(cv[...])
    sk_high, sk_low = split2(skt[...])
    n_targets = cv.shape[0]
    first = mm(jnp.concatenate([coef_high, coef_low], axis=0), sk_high)
    predicted = first[:n_targets] + first[n_targets:] + mm(coef_high, sk_low)
    pred_send[...] = predicted.reshape(n_targets // 8, 8, structs)
    pred_recv[p] = pred_send[q]

    def exchange(src_slot, dst_slot, peer):
        return pltpu.make_async_remote_copy(
            src_ref=pred_send.at[src_slot],
            dst_ref=pred_recv.at[dst_slot],
            send_sem=late_sem.at[0],
            recv_sem=late_sem.at[1],
            device_id=peer,
            device_id_type=MESH,
        )

    n_plane = pred_recv.shape[0]

    far = sorted(range(1, n_plane), key=lambda i: -sum(min(v, NX - v) for v in (i // 2 // NX, i // 2 % NX)))
    for i in far:
        yi, xi = chip(i // 2 // NX, i // 2 % NX)
        peer = (yi * NX + xi) * 2 + (c if i % 2 == 0 else 1 - c)
        exchange(lax.div(peer, 4), p, (z, peer)).start()

    locals_[5].wait()
    settle(tz.at[pl.ds(0, NZ - 1)], late_sem.at[9], False)
    wanted = destv[pl.ds(z, 1), :]
    home = jnp.zeros((48, structs), F32)
    for owner in range(NZ):
        spots = lax.broadcasted_iota(jnp.int32, (structs, structs), 0) + owner * structs
        pick = jnp.where(spots == wanted, 1.0, 0.0).astype(BF16)
        home = home + mm(jnp.concatenate(split3(tz[owner]), axis=0), pick)
    home = (home[0:16] + home[16:32]) + home[32:48]
    turned = skt[...].T
    sk_high, sk_low = split2(turned)
    sht[...] = sk_high
    slt[...] = sk_low

    settle(pred_recv.at[pl.ds(0, n_plane - 1)], late_sem.at[1], False)
    summed = jnp.sum(pred_recv[...], axis=0)
    resid = home[8:16] * (summed - home[0:8])
    tiles[q] = resid

    def tile_copy(yi, xi):
        return pltpu.make_async_remote_copy(
            src_ref=tiles.at[q],
            dst_ref=tiles.at[q],
            send_sem=late_sem.at[2],
            recv_sem=late_sem.at[3],
            device_id=(z, (yi * NX + xi) * 2 + c),
            device_id_type=MESH,
        )

    for dy in (2, 1, 3, 0):
        yi = lax.rem(y + dy, NX)
        tile_copy(yi, NX - 1 - x).start()
        if dy:
            tile_copy(yi, x).start()
    mine = lax.rem(p, 4)
    out = resid[0:2]
    for j in range(1, 4):
        out = jnp.where(mine == j, resid[2 * j : 2 * j + 2], out)
    res_ref[...] = out
    settle(tiles.at[pl.ds(0, 7)], late_sem.at[3], False)

    res_high, res_low = split2(tiles[...].reshape(n_targets, structs))
    first = mm(jnp.concatenate([res_high, res_low], axis=0), sht[...])
    grads = first[:n_targets] + first[n_targets:] + mm(res_high, slt[...])
    grads = grads * (1.0 / (structs * NZ))
    share_rows = n_targets // NZ
    largest = jnp.max(jnp.max(jnp.abs(grads), axis=0, keepdims=True), axis=1, keepdims=True)
    largest = jnp.maximum(jnp.broadcast_to(largest, (1, 128)), 1e-30)
    step_send[...] = largest * (1.0 / CODES**2)
    to_one = jnp.broadcast_to(1.0 / largest, (n_targets, 128))
    to_one = jnp.concatenate([to_one] * (pivots // 128), axis=1)
    codes = jnp.floor(jnp.sqrt(jnp.abs(grads) * to_one) * CODES + 0.5)
    codes = jnp.where(grads < 0, -codes, codes).astype(jnp.int32)
    for owner in range(NZ):
        part = codes[owner * share_rows : (owner + 1) * share_rows]
        part = jnp.concatenate([part[:, k * 256 : (k + 1) * 256] for k in range(pivots // 256)], axis=0)
        grad_send[owner] = part.astype(jnp.int16)
    grad_recv[z] = grad_send[z]
    step_recv[z] = step_send[...]

    def send_grad(i, carry):
        peer = lax.rem(z + i, NZ)
        for src, dst, sem in (
            (grad_send.at[peer], grad_recv.at[z], 4),
            (step_send, step_recv.at[z], 6),
        ):
            pltpu.make_async_remote_copy(
                src_ref=src,
                dst_ref=dst,
                send_sem=late_sem.at[sem],
                recv_sem=late_sem.at[sem + 1],
                device_id=(peer, p),
                device_id_type=MESH,
            ).start()
        return carry

    for i in (8, 7, 9, 6, 10, 5, 11, 4, 12, 3, 13, 2, 14, 1, 15):
        send_grad(i, 0)

    settle(gathered.at[0, :, c], own_sem, True)
    settle(gathered.at[0:2, 0:3, c], line_sem, True)
    settle(gathered.at[0, 0, c], half_sem.at[0], True)
    settle(gathered.at[0, :, c], half_sem.at[1], True)
    settle(gathered.at[:, :, c], part_send_sem, True)
    settle(tz.at[pl.ds(0, NZ - 1)], late_sem.at[8], True)
    settle(pred_recv.at[pl.ds(0, n_plane - 1)], late_sem.at[0], True)
    settle(tiles.at[pl.ds(0, 7)], late_sem.at[2], True)
    settle(grad_recv.at[pl.ds(0, NZ - 1)], late_sem.at[5], False)
    settle(step_recv.at[pl.ds(0, NZ - 1)], late_sem.at[7], False)
    settle(step_recv.at[pl.ds(0, NZ - 1)], late_sem.at[6], True)
    total = jnp.zeros(grad_recv.shape[1:], F32)
    for src in range(NZ):
        scale = step_recv[src]
        scale = jnp.concatenate([scale, scale], axis=1)
        code = grad_recv[src].astype(jnp.int32).astype(F32)
        total = total + (code * jnp.abs(code)) * scale
    for k in range(pivots // 256):
        grad_ref[:, k * 256 : (k + 1) * 256] = total[k * share_rows : (k + 1) * share_rows]
    settle(grad_send.at[pl.ds(0, NZ - 1)], late_sem.at[4], True)


def store(res_ref, grad_ref, res_out, grad_out, sem):
    copies = [
        pltpu.make_async_copy(res_ref, res_out, sem.at[0]),
        pltpu.make_async_copy(grad_ref, grad_out, sem.at[1]),
    ]
    for copy in copies:
        copy.start()
    for copy in copies:
        copy.wait()


def on_device(descriptors, pivot_desc, coeffs, seg_ids, dest, targets, weights):
    atoms, rows = descriptors.shape
    pivots, width = pivot_desc.shape
    structs, n_targets = targets.shape
    any_spec = pl.BlockSpec(memory_space=pltpu.HBM)
    vmem_spec = pl.BlockSpec(memory_space=pltpu.VMEM)
    dma = pltpu.SemaphoreType.DMA
    res, grad = pl.pallas_call(
        kernel,
        out_shape=(
            pltpu.VMEM((n_targets // 32, structs), F32),
            pltpu.VMEM((n_targets // NZ, pivots), F32),
        ),
        in_specs=[any_spec] * 7,
        out_specs=(vmem_spec, vmem_spec),
        scratch_shapes=[
            pltpu.VMEM((NX, NX, 2, rows, atoms), BF16),
            pltpu.VMEM((pivots, width), BF16),
            pltpu.VMEM((n_targets, pivots), F32),
            pltpu.VMEM((1, atoms), jnp.int32),
            pltpu.VMEM((NZ, structs), jnp.int32),
            pltpu.VMEM((n_targets // 8, 8, structs), F32),
            pltpu.VMEM((1, structs), F32),
            pltpu.VMEM((pivots, 128), F32),
            pltpu.VMEM((atoms, structs), BF16),
            pltpu.VMEM((pivots, structs), F32),
            pltpu.VMEM((structs, pivots), BF16),
            pltpu.VMEM((structs, pivots), BF16),
            pltpu.VMEM((NZ, 16, structs), F32),
            pltpu.VMEM((n_targets // 8, 8, structs), F32),
            pltpu.VMEM((32, 8, structs), F32),
            pltpu.VMEM((n_targets // 8, 8, structs), F32),
            pltpu.VMEM((NZ, 16, 256), jnp.int16),
            pltpu.VMEM((NZ, 16, 256), jnp.int16),
            pltpu.VMEM((1, 128), F32),
            pltpu.VMEM((NZ, 1, 128), F32),
            pltpu.VMEM((8, atoms), F32),
            pltpu.VMEM((pivots, atoms), F32),
            dma((7,)),
            dma,
            dma,
            dma((2,)),
            dma,
            dma((20, NB)),
            dma((5,)),
            pltpu.SemaphoreType.REGULAR((3,)),
            dma((10,)),
        ],
        compiler_params=pltpu.CompilerParams(
            collective_id=0, has_side_effects=True, vmem_limit_bytes=60 * 1024 * 1024
        ),
        name="fit_gradient",
    )(
        descriptors.T,
        pivot_desc,
        coeffs.T,
        seg_ids,
        dest.reshape(NZ, structs),
        targets.T.reshape(n_targets // 8, 8, structs),
        weights.reshape(1, structs),
    )
    res, grad = pl.pallas_call(
        store,
        out_shape=(
            jax.ShapeDtypeStruct(res.shape, F32),
            jax.ShapeDtypeStruct(grad.shape, F32),
        ),
        in_specs=[vmem_spec, vmem_spec],
        out_specs=(any_spec, any_spec),
        scratch_shapes=[dma((2,))],
        name="store_results",
    )(
        pltpu.with_memory_space_constraint(res, pltpu.VMEM),
        pltpu.with_memory_space_constraint(grad, pltpu.VMEM),
    )
    return res.T, grad


def solution(mesh):
    placed = (
        P("atoms", "pivots"),
        P("pivots", None),
        P("pivots", None),
        P("atoms", None),
        P(),
        P("atoms", None),
        P("atoms"),
    )
    return jax.shard_map(
        on_device,
        mesh=mesh,
        in_specs=placed,
        out_specs=(P("atoms", "pivots"), P("atoms", "pivots")),
        check_vma=False,
    )
```
